32 devices in a mesh: user: 8 (over z, y), item: 4 (over x, core).
Axes of the slice: x: 2, y: 2, z: 4, core: 2. Of those that a mesh axis runs over, the one named last changes fastest.
Arguments:
- v_start: bfloat16 [32768, 64], P(('user', 'item')), may hold values from -6 to 6
- locked: bfloat16 [32768, 32], P(('user', 'item')), may hold values from -0.0625 to 0.0625
- tile_rows: int32 [32, 512], P(('user', 'item')), may hold values from 0 to 63, as said below
- tile_cols: int32 [32, 512], P(('user', 'item')), may hold values from 0 to 63
- tile_seeds: int32 [32, 512], P(('user', 'item')), may hold values from 0 to 1048575
- tile_count: int32 [32, 1], P(('user', 'item')), may hold values from 128 to 512, as said below
Outputs:
- u_factor: bfloat16 [65536, 64], P(('user', 'item'))
- v_next: float32 [32768, 64], P(('user', 'item'))
The draws below stay inside these ranges and needn't reach their ends.
Inputs may be any that keep to these rules, and one draw needn't show every extreme that they name: `tile_count`: at most 512 live slots a device, and one device holds exactly 512. `tile_rows`: A device's slots name distinct (row, column) pairs.
All inputs are finite; a program needn't handle non-finite values.
Results may differ from the reference program's by a relative error of at most 0.0049.
Values may be sent and summed in bfloat16 or wider, within the bound.
A program may use at most 64 MiB of HBM per device.

```python
import jax
import jax.numpy as jnp
from jax import lax

TILE = 128
K = 64
LOCK = 32
RB = 64
CAP = 512
CB = 64
SHARD = 1024
USERS = 65536
ITEMS = 32768
N_USER = 8
N_ITEM = 4


def slot_positions(key):
    keys = jax.random.split(jax.random.fold_in(key, 7), N_USER * N_ITEM)
    return jax.vmap(lambda k: jax.random.permutation(k, RB * CB)[:CAP])(keys).astype(jnp.int32)


def draw_tile_rows(key, part):
    return slot_positions(key) // CB


def draw_tile_cols(key, part):
    return slot_positions(key) % CB


def draw_tile_seeds(key, part):
    return jax.random.randint(jax.random.fold_in(key, 17), (N_USER * N_ITEM, CAP), 0, 1048576, dtype=jnp.int32)


def draw_tile_count(key, part):
    total = N_USER * N_ITEM
    counts = jax.random.randint(jax.random.fold_in(key, 11), (total,), CAP // 4, CAP // 2 + 1, dtype=jnp.int32)
    busiest = jax.random.randint(jax.random.fold_in(key, 13), (), 0, total, dtype=jnp.int32)
    counts = jnp.where(jnp.arange(total, dtype=jnp.int32) == busiest, CAP, counts)
    return counts.reshape(total, 1)


def block_levels(stream_key, shape, pieces, least, top_value):
    factor_of = 1.0
    for axis_at, shards_of in pieces:
        heights = jax.random.uniform(jax.random.fold_in(jax.random.fold_in(stream_key, 6), axis_at), (shards_of,), jnp.float32, least / len(pieces), top_value / len(pieces))
        factor_of = factor_of * jnp.repeat(jnp.exp(heights), shape[axis_at] // shards_of).reshape((-1,) + (1,) * (len(shape) - 1 - axis_at))
    return factor_of


def normal_values(stream_key, extent, deviation, bound, cuts=(), kind=jnp.bfloat16):
    array = jax.random.normal(stream_key, extent, jnp.float32) * deviation
    if len(cuts) > 0:
        array = block_levels(stream_key, extent, cuts, -0.22, 0.18) * array
    return jnp.clip(array, min=-bound, max=bound).astype(kind)


def setup_inputs(seed: int = 0) -> dict:
    key_list = jax.random.split(jax.random.key(seed), 7)
    return {
        "v_start": normal_values(key_list[0], (ITEMS, K), 1.0, 6.0, ((0, 32),)),
        "locked": normal_values(key_list[1], (ITEMS, LOCK), (ITEMS // 4) ** -0.5, 0.0625, ((0, 32),)),
        "tile_rows": draw_tile_rows(jax.random.fold_in(key_list[6], 71), 0),
        "tile_cols": draw_tile_cols(jax.random.fold_in(key_list[6], 71), 0),
        "tile_seeds": draw_tile_seeds(jax.random.fold_in(key_list[6], 71), 0),
        "tile_count": draw_tile_count(jax.random.fold_in(key_list[6], 71), 0),
    }


tile_batch = 16

def tile_values(seeds):
    rowpos = lax.broadcasted_iota(jnp.int32, (TILE, TILE), 0)
    colpos = lax.broadcasted_iota(jnp.int32, (TILE, TILE), 1)
    hashed = (rowpos * TILE + colpos)[None, :, :] * 40503 + seeds[:, None, None] * 9973
    hashed = jnp.bitwise_xor(hashed, jnp.right_shift(hashed, 13))
    hashed = hashed * 1597334677
    hashed = jnp.bitwise_xor(hashed, jnp.right_shift(hashed, 16))
    levels = jnp.bitwise_and(jnp.right_shift(hashed, 8), 255) - 128
    return (levels.astype(jnp.float32) * (1.0 / 1024.0)).astype(jnp.bfloat16)

def group_slice(rows, cols, seeds, count, start):
    grows = lax.dynamic_slice_in_dim(rows, start, tile_batch)
    gcols = lax.dynamic_slice_in_dim(cols, start, tile_batch)
    gseeds = lax.dynamic_slice_in_dim(seeds, start, tile_batch)
    valid = start + jnp.arange(tile_batch, dtype=jnp.int32) < count
    return (grows, gcols, gseeds, valid)

def forward_pass(rows, cols, seeds, count, vblocks):

    def step(g, upart):
        grows, gcols, gseeds, valid = group_slice(rows, cols, seeds, count, g * tile_batch)
        tiles = tile_values(gseeds).astype(jnp.float32)
        prod = jnp.einsum('gab,gbk->gak', tiles, vblocks[gcols].astype(jnp.float32), precision=lax.Precision.HIGHEST)
        prod = jnp.where(valid[:, None, None], prod, 0.0)
        return upart.at[grows].add(prod)
    steps = (count + tile_batch - 1) // tile_batch
    return lax.fori_loop(0, steps, step, jnp.zeros((RB, TILE, K), jnp.float32))

def backward_pass(rows, cols, seeds, count, ublocks):

    def step(g, wpart):
        grows, gcols, gseeds, valid = group_slice(rows, cols, seeds, count, g * tile_batch)
        tiles = tile_values(gseeds).astype(jnp.float32)
        prod = jnp.einsum('gab,gak->gbk', tiles, ublocks[grows].astype(jnp.float32), precision=lax.Precision.HIGHEST)
        prod = jnp.where(valid[:, None, None], prod, 0.0)
        return wpart.at[gcols].add(prod)
    steps = (count + tile_batch - 1) // tile_batch
    return lax.fori_loop(0, steps, step, jnp.zeros((CB, TILE, K), jnp.float32))

def reference(v_start, locked, tile_rows, tile_cols, tile_seeds, tile_count):
    high = lax.Precision.HIGHEST
    lockf = locked.astype(jnp.float32)
    proj = jnp.dot(locked.T, v_start, preferred_element_type=jnp.float32)
    deflated = (v_start.astype(jnp.float32) - jnp.dot(lockf, proj, precision=high)).astype(jnp.bfloat16)
    dshards = deflated.reshape(N_USER, N_ITEM, SHARD, K)
    devices = jnp.arange(N_USER * N_ITEM, dtype=jnp.int32)

    def forward_dev(uacc, dev):
        uidx = dev // N_ITEM
        iidx = dev % N_ITEM
        vblocks = lax.dynamic_index_in_dim(dshards, iidx, 1, keepdims=False).reshape(CB, TILE, K)
        part = forward_pass(tile_rows[dev], tile_cols[dev], tile_seeds[dev], tile_count[dev, 0], vblocks)
        current = lax.dynamic_index_in_dim(uacc, uidx, 0, keepdims=False)
        return (lax.dynamic_update_index_in_dim(uacc, current + part, uidx, 0), None)
    uacc, _ = lax.scan(forward_dev, jnp.zeros((N_USER, RB, TILE, K), jnp.float32), devices)
    ublocks_all = uacc.astype(jnp.bfloat16)
    u_factor = ublocks_all.reshape(USERS, K)

    def backward_dev(wacc, dev):
        uidx = dev // N_ITEM
        iidx = dev % N_ITEM
        ublocks = lax.dynamic_index_in_dim(ublocks_all, uidx, 0, keepdims=False)
        part = backward_pass(tile_rows[dev], tile_cols[dev], tile_seeds[dev], tile_count[dev, 0], ublocks)
        return (wacc.at[iidx].add(part.reshape(CB * TILE, K)), None)
    wacc, _ = lax.scan(backward_dev, jnp.zeros((N_ITEM, CB * TILE, K), jnp.float32), devices)
    back = wacc.reshape(N_ITEM, N_USER, SHARD, K).transpose(1, 0, 2, 3).reshape(ITEMS, K)
    proj2 = jnp.dot(lockf.T, back, precision=high)
    rest = back - jnp.dot(lockf, proj2, precision=high)
    colsq = lax.optimization_barrier(jnp.sum(rest * rest, axis=0))
    v_next = rest / jnp.sqrt(colsq / ITEMS + 1e-06)
    return (u_factor, v_next)
```

```python
import jax
import jax.numpy as jnp
from jax import lax
from jax.experimental import pallas as pl
from jax.experimental.pallas import tpu as pltpu
from jax.sharding import PartitionSpec as P

TILE = 128
RB = 64
GROUP = 16
SCALE = 1.0 / 1024.0
HIGH = lax.Precision.HIGHEST
NT = (((1,), (1,)), ((), ()))
NN = (((1,), (0,)), ((), ()))


def forward_kernel(rows, cols, seeds, count, v_ref, tiles_ref, u_ref, acc):
    g = pl.program_id(0)
    blocks = u_ref.shape[0]

    @pl.when(g == 0)
    def _():
        acc[...] = jnp.zeros_like(acc)

    @pl.when(g * GROUP < count[0, 0])
    def _():
        a = lax.broadcasted_iota(jnp.int32, (TILE, TILE), 0)
        b = lax.broadcasted_iota(jnp.int32, (TILE, TILE), 1)
        base = (a * TILE + b) * 40503
        for j in range(GROUP):
            s = g * GROUP + j
            h = base + seeds[0, s] * 9973
            h = h ^ (h >> 13)
            h = h * 1597334677
            h = h ^ (h >> 16)
            tile = (((h >> 8) & 255) - 128).astype(jnp.float32).astype(jnp.bfloat16)
            tiles_ref[j] = tile
            row = jnp.where(s < count[0, 0], rows[0, s], blocks)
            acc[row] += lax.dot_general(
                v_ref[cols[0, s]], tile, NT, preferred_element_type=jnp.float32
            )

    @pl.when(g == pl.num_programs(0) - 1)
    def _():
        u_ref[...] = (acc[:blocks] * SCALE).astype(u_ref.dtype)


def backward_kernel(rows, cols, count, u_ref, tiles_ref, w_ref, acc):
    g = pl.program_id(0)
    blocks = w_ref.shape[0]

    @pl.when(g == 0)
    def _():
        acc[...] = jnp.zeros_like(acc)

    @pl.when(g * GROUP < count[0, 0])
    def _():
        for j in range(GROUP):
            s = g * GROUP + j
            col = jnp.where(s < count[0, 0], cols[0, s], blocks)
            acc[col] += lax.dot_general(
                u_ref[rows[0, s]], tiles_ref[j], NN, preferred_element_type=jnp.float32
            )

    @pl.when(g == pl.num_programs(0) - 1)
    def _():
        w_ref[...] = (acc[:blocks] * SCALE).astype(w_ref.dtype)


def tile_spec(count_at):
    def index(g, *refs):
        last = lax.div(refs[count_at][0, 0] + (GROUP - 1), GROUP) - 1
        return (jnp.minimum(g, last), 0, 0)

    return pl.BlockSpec((GROUP, TILE, TILE), index)


def whole_spec(shape):
    return pl.BlockSpec(shape, lambda g, *refs: (0,) * len(shape))


def forward(rows, cols, seeds, count, vblocks, dtype):
    nblocks, width, tile = vblocks.shape
    slots = rows.shape[1]
    out = (RB, width, tile)
    return pl.pallas_call(
        forward_kernel,
        name="forward",
        out_shape=(
            jax.ShapeDtypeStruct((slots, tile, tile), jnp.bfloat16),
            jax.ShapeDtypeStruct(out, dtype),
        ),
        grid_spec=pltpu.PrefetchScalarGridSpec(
            num_scalar_prefetch=4,
            grid=(slots // GROUP,),
            in_specs=[whole_spec(vblocks.shape)],
            out_specs=[tile_spec(3), whole_spec(out)],
            scratch_shapes=[pltpu.VMEM((RB + 1, width, tile), jnp.float32)],
        ),
        compiler_params=pltpu.CompilerParams(vmem_limit_bytes=32 << 20),
    )(rows, cols, seeds, count, vblocks)


def backward(rows, cols, count, ublocks, tiles, nblocks, dtype):
    width, tile = ublocks.shape[1:]
    slots = rows.shape[1]
    out = (nblocks, width, tile)
    return pl.pallas_call(
        backward_kernel,
        name="backward",
        out_shape=jax.ShapeDtypeStruct(out, dtype),
        grid_spec=pltpu.PrefetchScalarGridSpec(
            num_scalar_prefetch=3,
            grid=(slots // GROUP,),
            in_specs=[whole_spec(ublocks.shape), tile_spec(2)],
            out_specs=whole_spec(out),
            scratch_shapes=[pltpu.VMEM((nblocks + 1, width, tile), jnp.float32)],
        ),
        compiler_params=pltpu.CompilerParams(vmem_limit_bytes=32 << 20),
    )(rows, cols, count, ublocks, tiles)


def blocks_of(x):
    return x.reshape(-1, TILE, x.shape[1]).transpose(0, 2, 1)


def rows_of(blocks):
    return blocks.transpose(0, 2, 1).reshape(-1, blocks.shape[1])


def on_device(v_start, locked, tile_rows, tile_cols, tile_seeds, tile_count):
    both = ("user", "item")
    lockf = locked.astype(jnp.float32)
    nlock = locked.shape[1]
    n_user, n_item = lax.axis_size("user"), lax.axis_size("item")
    slab = v_start.shape[0] * n_user
    stats = jnp.dot(
        locked.T, jnp.concatenate([v_start, locked], axis=1), preferred_element_type=jnp.float32
    )
    stats = lax.psum(stats, both)
    proj, gram = stats[:, :-nlock], stats[:, -nlock:]
    deflated = (v_start.astype(jnp.float32) - jnp.dot(lockf, proj, precision=HIGH)).astype(
        jnp.bfloat16
    )
    vslab = lax.all_gather(deflated, "user", axis=0, tiled=True)
    tiles, upart = forward(
        tile_rows, tile_cols, tile_seeds, tile_count, blocks_of(vslab), jnp.float32
    )
    ublocks = lax.psum(upart, "item").astype(jnp.bfloat16)
    per = RB // n_item
    u_factor = rows_of(lax.dynamic_slice_in_dim(ublocks, lax.axis_index("item") * per, per, 0))
    wpart = backward(
        tile_rows, tile_cols, tile_count, ublocks, tiles, slab // TILE, jnp.float32
    )
    back = lax.psum_scatter(rows_of(wpart), "user", scatter_dimension=0, tiled=True)
    sums = jnp.concatenate(
        [jnp.dot(lockf.T, back, precision=HIGH), jnp.sum(back * back, axis=0)[None]], axis=0
    )
    sums = lax.psum(sums, both)
    proj2, backsq = sums[:-1], sums[-1]
    rest = back - jnp.dot(lockf, proj2, precision=HIGH)
    crossed = jnp.dot(gram, proj2, precision=HIGH) - 2.0 * proj2
    colsq = jnp.maximum(backsq + jnp.sum(proj2 * crossed, axis=0), 0.0)
    v_next = rest / jnp.sqrt(colsq / (slab * n_item) + 1e-06)
    return (u_factor, v_next)


def solution(mesh):
    spec = P(("user", "item"), None)
    return jax.shard_map(
        on_device, mesh=mesh, in_specs=(spec,) * 6, out_specs=(spec, spec), check_vma=False
    )
```

```python
import functools

import jax
import jax.numpy as jnp
from jax import lax
from jax.experimental import pallas as pl
from jax.experimental.pallas import tpu as pltpu
from jax.sharding import PartitionSpec as P

TILE = 128
RB = 64
GROUP = 16
SCALE = 1.0 / 1024.0
HIGH = lax.Precision.HIGHEST
NT = (((1,), (1,)), ((), ()))
NN = (((1,), (0,)), ((), ()))


def forward_kernel(rows, cols, seeds, count, v_ref, tiles_ref, u_ref, acc):
    g = pl.program_id(0)
    blocks = u_ref.shape[0]

    @pl.when(g == 0)
    def _():
        acc[...] = jnp.zeros_like(acc)

    @pl.when(g * GROUP < count[0, 0])
    def _():
        a = lax.broadcasted_iota(jnp.int32, (TILE, TILE), 0)
        b = lax.broadcasted_iota(jnp.int32, (TILE, TILE), 1)
        base = (a * TILE + b) * 40503
        for j in range(GROUP):
            s = g * GROUP + j
            h = base + seeds[0, s] * 9973
            h = h ^ (h >> 13)
            h = h * 1597334677
            h = h ^ (h >> 16)
            tile = (((h >> 8) & 255) - 128).astype(jnp.float32).astype(jnp.bfloat16)
            tiles_ref[j] = tile
            row = jnp.where(s < count[0, 0], rows[0, s], blocks)
            acc[row] += lax.dot_general(
                v_ref[cols[0, s]], tile, NT, preferred_element_type=jnp.float32
            )

    @pl.when(g == pl.num_programs(0) - 1)
    def _():
        u_ref[...] = (acc[:blocks] * SCALE).astype(u_ref.dtype)


def backward_kernel(rows, cols, count, u_ref, tiles_ref, w_ref, acc):
    g = pl.program_id(0)
    blocks = w_ref.shape[0]

    @pl.when(g == 0)
    def _():
        acc[...] = jnp.zeros_like(acc)

    @pl.when(g * GROUP < count[0, 0])
    def _():
        for j in range(GROUP):
            s = g * GROUP + j
            col = jnp.where(s < count[0, 0], cols[0, s], blocks)
            acc[col] += lax.dot_general(
                u_ref[rows[0, s]], tiles_ref[j], NN, preferred_element_type=jnp.float32
            )

    @pl.when(g == pl.num_programs(0) - 1)
    def _():
        w_ref[...] = (acc[:blocks] * SCALE).astype(w_ref.dtype)


def tile_spec(count_at):
    def index(g, *refs):
        last = lax.div(refs[count_at][0, 0] + (GROUP - 1), GROUP) - 1
        return (jnp.minimum(g, last), 0, 0)

    return pl.BlockSpec((GROUP, TILE, TILE), index)


def whole_spec(shape):
    return pl.BlockSpec(shape, lambda g, *refs: (0,) * len(shape))


def forward(rows, cols, seeds, count, vblocks, dtype):
    nblocks, width, tile = vblocks.shape
    slots = rows.shape[1]
    out = (RB, width, tile)
    return pl.pallas_call(
        forward_kernel,
        name="forward",
        out_shape=(
            jax.ShapeDtypeStruct((slots, tile, tile), jnp.bfloat16),
            jax.ShapeDtypeStruct(out, dtype),
        ),
        grid_spec=pltpu.PrefetchScalarGridSpec(
            num_scalar_prefetch=4,
            grid=(slots // GROUP,),
            in_specs=[whole_spec(vblocks.shape)],
            out_specs=[tile_spec(3), whole_spec(out)],
            scratch_shapes=[pltpu.VMEM((RB + 1, width, tile), jnp.float32)],
        ),
        compiler_params=pltpu.CompilerParams(vmem_limit_bytes=32 << 20),
    )(rows, cols, seeds, count, vblocks)


def backward(rows, cols, count, ublocks, tiles, nblocks, dtype):
    width, tile = ublocks.shape[1:]
    slots = rows.shape[1]
    out = (nblocks, width, tile)
    return pl.pallas_call(
        backward_kernel,
        name="backward",
        out_shape=jax.ShapeDtypeStruct(out, dtype),
        grid_spec=pltpu.PrefetchScalarGridSpec(
            num_scalar_prefetch=3,
            grid=(slots // GROUP,),
            in_specs=[whole_spec(ublocks.shape), tile_spec(2)],
            out_specs=whole_spec(out),
            scratch_shapes=[pltpu.VMEM((nblocks + 1, width, tile), jnp.float32)],
        ),
        compiler_params=pltpu.CompilerParams(vmem_limit_bytes=32 << 20),
    )(rows, cols, count, ublocks, tiles)


def blocks_of(x):
    return x.reshape(-1, TILE, x.shape[1]).transpose(0, 2, 1)


def rows_of(blocks):
    return blocks.transpose(0, 2, 1).reshape(-1, blocks.shape[1])


MESH = pl.DeviceIdType.MESH
CHUNKS = 4


def peers(axis):
    n, me = lax.axis_size(axis), lax.axis_index(axis)
    return [{axis: lax.rem(me + o, n)} for o in range(1, n)]


def meet(devices):
    barrier = pltpu.get_barrier_semaphore()
    for device in devices:
        pl.semaphore_signal(barrier, inc=1, device_id=device, device_id_type=MESH)
    pl.semaphore_wait(barrier, len(devices))


def remote(src, dst, send, recv, device):
    return pltpu.make_async_remote_copy(
        src_ref=src, dst_ref=dst, send_sem=send, recv_sem=recv, device_id=device,
        device_id_type=MESH,
    )


def sum_over(axis, value, slots, send, recv):
    n, me = lax.axis_size(axis), lax.axis_index(axis)
    slots[me] = value
    copies = [
        remote(slots.at[me], slots.at[me], send.at[o], recv.at[o], device)
        for o, device in enumerate(peers(axis))
    ]
    for copy in copies:
        copy.start()
    for copy in copies:
        copy.wait()
    total = slots[0]
    for i in range(1, n):
        total = total + slots[i]
    return total


def gather_kernel(cat_ref, v_ref, stats_ref, slots_i, slots_u, si, ri, su, ru, sg, rg):
    nlock = stats_ref.shape[0]
    width = v_ref.shape[1]
    meet(peers("item") + peers("user"))
    lock = cat_ref[:nlock]
    stats = lax.dot_general(lock, cat_ref[...], NT, preferred_element_type=jnp.float32)
    stats = sum_over("item", stats, slots_i, si, ri)
    stats = sum_over("user", stats, slots_u, su, ru)
    stats_ref[...] = stats
    projt = stats.T[nlock : nlock + width]
    own = cat_ref.shape[1] // TILE
    first = lax.axis_index("user") * own
    for j in range(own):
        at = slice(j * TILE, (j + 1) * TILE)
        v = cat_ref[nlock : nlock + width, at].astype(jnp.float32)
        part = jnp.dot(projt, cat_ref[:nlock, at].astype(jnp.float32), precision=HIGH)
        v_ref[first + j] = (v - part).astype(v_ref.dtype)
    mine = v_ref.at[pl.ds(first, own)]
    copies = [
        remote(mine, mine, sg.at[o], rg.at[o], device)
        for o, device in enumerate(peers("user"))
    ]
    for copy in copies:
        copy.start()
    for copy in copies:
        copy.wait()


def user_sum_kernel(part_ref, u_ref, near, pair, far, sem):
    me = lax.axis_index("item")
    side = lax.rem(me, 2)
    sibling = {"item": me + 1 - 2 * side}
    across = {"item": lax.rem(me + 2, 4)}
    half = part_ref.shape[0] // 2
    size = half // CHUNKS
    meet([sibling, across])

    def copies(step, src, src_at, dst, dst_at, device):
        return [
            remote(
                src.at[pl.ds(src_at + k * size, size)],
                dst.at[pl.ds(dst_at + k * size, size)],
                sem.at[2 * step, k],
                sem.at[2 * step + 1, k],
                device,
            )
            for k in range(CHUNKS)
        ]

    give = copies(0, part_ref, (1 - side) * half, near, 0, sibling)
    swap = copies(1, pair, 0, far, 0, across)
    back = copies(2, u_ref, side * half, u_ref, side * half, sibling)
    for copy in give:
        copy.start()
    for k in range(CHUNKS):
        give[k].wait_recv()
        at = pl.ds(k * size, size)
        own = part_ref[pl.ds(side * half + k * size, size)].astype(jnp.float32)
        pair[at] = (own + near[at].astype(jnp.float32)).astype(pair.dtype)
        swap[k].start()
    for k in range(CHUNKS):
        swap[k].wait_recv()
        at = pl.ds(k * size, size)
        total = pair[at].astype(jnp.float32) + far[at].astype(jnp.float32)
        u_ref[pl.ds(side * half + k * size, size)] = total.astype(u_ref.dtype)
        back[k].start()
    for k in range(CHUNKS):
        give[k].wait_send()
        swap[k].wait_send()
        back[k].wait()


def finish_kernel(
    items, part_ref, lock_ref, stats_ref, v_ref, land, slots_i, slots_u, s, r, si, ri, su, ru
):
    nlock = stats_ref.shape[0]
    own, width, tile = land.shape[1:]
    n, me = lax.axis_size("user"), lax.axis_index("user")
    meet(peers("item") + peers("user"))
    copies = [
        remote(
            part_ref.at[pl.ds(device["user"] * own, own)], land.at[me], s.at[o], r.at[o], device
        )
        for o, device in enumerate(peers("user"))
    ]
    for copy in copies:
        copy.start()
    land[me] = part_ref[pl.ds(me * own, own)]
    for copy in copies:
        copy.wait()
    back, sums = [], jnp.zeros((width, tile), jnp.float32)
    square = jnp.zeros((width, tile), jnp.float32)
    for j in range(own):
        b = land[0, j].astype(jnp.float32)
        for i in range(1, n):
            b = b + land[i, j].astype(jnp.float32)
        back.append(b)
        square = square + b * b
        lock = lock_ref[:, j * tile : (j + 1) * tile].astype(jnp.float32)
        sums = sums + lax.dot_general(
            b, lock, NT, precision=HIGH, preferred_element_type=jnp.float32
        )
    lane = lax.broadcasted_iota(jnp.int32, (width, tile), 1)
    sums = jnp.where(lane == nlock, jnp.sum(square, axis=1, keepdims=True), sums)
    sums = sum_over("item", sums, slots_i, si, ri)
    sums = sum_over("user", sums, slots_u, su, ru)
    proj2, backsq = sums[:, :nlock], sums[:, nlock : nlock + 1]
    gram = stats_ref[:, :nlock]
    crossed = jnp.dot(proj2, gram, precision=HIGH) - 2.0 * proj2
    colsq = backsq + jnp.sum(proj2 * crossed, axis=1, keepdims=True)
    scale = 1.0 / jnp.sqrt(jnp.maximum(colsq, 0.0) / items + 1e-06)
    for j in range(own):
        lock = lock_ref[:nlock, j * tile : (j + 1) * tile].astype(jnp.float32)
        rest = back[j] - jnp.dot(proj2, lock, precision=HIGH)
        v_ref[j * tile : (j + 1) * tile, :] = (rest * scale).T


def comm_call(kernel, name, key, out_shape, scratch, *args):
    vmem = pl.BlockSpec(memory_space=pltpu.VMEM)
    return pl.pallas_call(
        kernel,
        name=name,
        out_shape=out_shape,
        in_specs=[vmem] * len(args),
        out_specs=jax.tree.map(lambda _: vmem, out_shape),
        scratch_shapes=scratch,
        compiler_params=pltpu.CompilerParams(
            collective_id=key, has_side_effects=True, vmem_limit_bytes=32 << 20
        ),
    )(*args)


def sems(*shape):
    return pltpu.SemaphoreType.DMA(shape)


def remote_plan(v_start, locked, tile_rows, tile_cols, tile_seeds, tile_count):
    n_user, n_item = lax.axis_size("user"), lax.axis_size("item")
    shard, width = v_start.shape
    nlock = locked.shape[1]
    nblocks = shard * n_user // TILE
    pad = jnp.zeros((shard, TILE - nlock - width), v_start.dtype)
    cat = jnp.concatenate([locked, v_start, pad], axis=1).T
    slab = (nblocks, width, TILE)
    pair = [sems(n_item - 1)] * 2 + [sems(n_user - 1)] * 2
    vblocks, stats = comm_call(
        gather_kernel,
        "gather",
        0,
        (
            jax.ShapeDtypeStruct(slab, jnp.bfloat16),
            jax.ShapeDtypeStruct((nlock, TILE), jnp.float32),
        ),
        [
            pltpu.VMEM((n_item, nlock, TILE), jnp.float32),
            pltpu.VMEM((n_user, nlock, TILE), jnp.float32),
        ]
        + pair
        + [sems(n_user - 1)] * 2,
        cat,
    )
    tiles, upart = forward(tile_rows, tile_cols, tile_seeds, tile_count, vblocks, jnp.bfloat16)
    half = pltpu.VMEM((RB // 2, width, TILE), jnp.bfloat16)
    ublocks = comm_call(
        user_sum_kernel,
        "user_sum",
        1,
        jax.ShapeDtypeStruct((RB, width, TILE), jnp.bfloat16),
        [half, half, half, sems(6, CHUNKS)],
        upart,
    )
    wpart = backward(tile_rows, tile_cols, tile_count, ublocks, tiles, nblocks, jnp.bfloat16)
    per = RB // n_item
    u_factor = rows_of(lax.dynamic_slice_in_dim(ublocks, lax.axis_index("item") * per, per, 0))
    only = jnp.concatenate([locked, jnp.zeros((shard, TILE - nlock), locked.dtype)], axis=1).T
    v_next = comm_call(
        functools.partial(finish_kernel, float(shard * n_user * n_item)),
        "finish",
        2,
        jax.ShapeDtypeStruct((shard, width), jnp.float32),
        [
            pltpu.VMEM((n_user, nblocks // n_user, width, TILE), jnp.bfloat16),
            pltpu.VMEM((n_item, width, TILE), jnp.float32),
            pltpu.VMEM((n_user, width, TILE), jnp.float32),
        ]
        + [sems(n_user - 1)] * 2
        + pair,
        wpart,
        only,
        stats,
    )
    return (u_factor, v_next)


def on_device(v_start, locked, tile_rows, tile_cols, tile_seeds, tile_count):
    if v_start.shape[0] % TILE == 0 and lax.axis_size("item") == 4:
        return remote_plan(v_start, locked, tile_rows, tile_cols, tile_seeds, tile_count)
    both = ("user", "item")
    lockf = locked.astype(jnp.float32)
    nlock = locked.shape[1]
    n_user, n_item = lax.axis_size("user"), lax.axis_size("item")
    slab = v_start.shape[0] * n_user
    stats = jnp.dot(
        locked.T, jnp.concatenate([v_start, locked], axis=1), preferred_element_type=jnp.float32
    )
    stats = lax.psum(stats, both)
    proj, gram = stats[:, :-nlock], stats[:, -nlock:]
    deflated = (v_start.astype(jnp.float32) - jnp.dot(lockf, proj, precision=HIGH)).astype(
        jnp.bfloat16
    )
    vslab = lax.all_gather(deflated, "user", axis=0, tiled=True)
    tiles, upart = forward(
        tile_rows, tile_cols, tile_seeds, tile_count, blocks_of(vslab), jnp.float32
    )
    ublocks = lax.psum(upart, "item").astype(jnp.bfloat16)
    per = RB // n_item
    u_factor = rows_of(lax.dynamic_slice_in_dim(ublocks, lax.axis_index("item") * per, per, 0))
    wpart = backward(
        tile_rows, tile_cols, tile_count, ublocks, tiles, slab // TILE, jnp.float32
    )
    back = lax.psum_scatter(rows_of(wpart), "user", scatter_dimension=0, tiled=True)
    sums = jnp.concatenate(
        [jnp.dot(lockf.T, back, precision=HIGH), jnp.sum(back * back, axis=0)[None]], axis=0
    )
    sums = lax.psum(sums, both)
    proj2, backsq = sums[:-1], sums[-1]
    rest = back - jnp.dot(lockf, proj2, precision=HIGH)
    crossed = jnp.dot(gram, proj2, precision=HIGH) - 2.0 * proj2
    colsq = jnp.maximum(backsq + jnp.sum(proj2 * crossed, axis=0), 0.0)
    v_next = rest / jnp.sqrt(colsq / (slab * n_item) + 1e-06)
    return (u_factor, v_next)


def solution(mesh):
    spec = P(("user", "item"), None)
    return jax.shard_map(
        on_device, mesh=mesh, in_specs=(spec,) * 6, out_specs=(spec, spec), check_vma=False
    )
```

```python
import functools

import jax
import jax.numpy as jnp
from jax import lax
from jax.experimental import pallas as pl
from jax.experimental.pallas import tpu as pltpu
from jax.sharding import PartitionSpec as P

TILE = 128
RB = 64
GROUP = 16
SCALE = 1.0 / 1024.0
HIGH = lax.Precision.HIGHEST
NT = (((1,), (1,)), ((), ()))
NN = (((1,), (0,)), ((), ()))


def forward_kernel(rows, cols, seeds, count, v_ref, tiles_ref, u_ref, acc):
    g = pl.program_id(0)
    blocks = u_ref.shape[0]

    @pl.when(g == 0)
    def _():
        acc[...] = jnp.zeros_like(acc)

    @pl.when(g * GROUP < count[0, 0])
    def _():
        a = lax.broadcasted_iota(jnp.int32, (TILE, TILE), 0)
        b = lax.broadcasted_iota(jnp.int32, (TILE, TILE), 1)
        base = (a * TILE + b) * 40503
        for j in range(GROUP):
            s = g * GROUP + j
            h = base + seeds[0, s] * 9973
            h = h ^ (h >> 13)
            h = h * 1597334677
            h = h ^ (h >> 16)
            tile = (((h >> 8) & 255) - 128).astype(jnp.float32).astype(jnp.bfloat16)
            tiles_ref[j] = tile
            row = jnp.where(s < count[0, 0], rows[0, s], blocks)
            acc[row] += lax.dot_general(
                v_ref[cols[0, s]], tile, NT, preferred_element_type=jnp.float32
            )

    @pl.when(g == pl.num_programs(0) - 1)
    def _():
        u_ref[...] = (acc[:blocks] * SCALE).astype(u_ref.dtype)


def backward_kernel(rows, cols, count, u_ref, tiles_ref, w_ref, acc):
    g = pl.program_id(0)
    blocks = w_ref.shape[0]

    @pl.when(g == 0)
    def _():
        acc[...] = jnp.zeros_like(acc)

    @pl.when(g * GROUP < count[0, 0])
    def _():
        for j in range(GROUP):
            s = g * GROUP + j
            col = jnp.where(s < count[0, 0], cols[0, s], blocks)
            acc[col] += lax.dot_general(
                u_ref[rows[0, s]], tiles_ref[j], NN, preferred_element_type=jnp.float32
            )

    @pl.when(g == pl.num_programs(0) - 1)
    def _():
        w_ref[...] = (acc[:blocks] * SCALE).astype(w_ref.dtype)


def tile_spec(count_at):
    def index(g, *refs):
        last = lax.div(refs[count_at][0, 0] + (GROUP - 1), GROUP) - 1
        return (jnp.minimum(g, last), 0, 0)

    return pl.BlockSpec((GROUP, TILE, TILE), index)


def whole_spec(shape):
    return pl.BlockSpec(shape, lambda g, *refs: (0,) * len(shape))


def forward(rows, cols, seeds, count, vblocks, dtype):
    nblocks, width, tile = vblocks.shape
    slots = rows.shape[1]
    out = (RB, width, tile)
    return pl.pallas_call(
        forward_kernel,
        name="forward",
        out_shape=(
            jax.ShapeDtypeStruct((slots, tile, tile), jnp.bfloat16),
            jax.ShapeDtypeStruct(out, dtype),
        ),
        grid_spec=pltpu.PrefetchScalarGridSpec(
            num_scalar_prefetch=4,
            grid=(slots // GROUP,),
            in_specs=[whole_spec(vblocks.shape)],
            out_specs=[tile_spec(3), whole_spec(out)],
            scratch_shapes=[pltpu.VMEM((RB + 1, width, tile), jnp.float32)],
        ),
        compiler_params=pltpu.CompilerParams(vmem_limit_bytes=16 << 20),
    )(rows, cols, seeds, count, vblocks)


def backward(rows, cols, count, ublocks, tiles, nblocks, dtype):
    width, tile = ublocks.shape[1:]
    slots = rows.shape[1]
    out = (nblocks, width, tile)
    return pl.pallas_call(
        backward_kernel,
        name="backward",
        out_shape=jax.ShapeDtypeStruct(out, dtype),
        grid_spec=pltpu.PrefetchScalarGridSpec(
            num_scalar_prefetch=3,
            grid=(slots // GROUP,),
            in_specs=[whole_spec(ublocks.shape), tile_spec(2)],
            out_specs=whole_spec(out),
            scratch_shapes=[pltpu.VMEM((nblocks + 1, width, tile), jnp.float32)],
        ),
        compiler_params=pltpu.CompilerParams(vmem_limit_bytes=16 << 20),
    )(rows, cols, count, ublocks, tiles)


def blocks_of(x):
    return x.reshape(-1, TILE, x.shape[1]).transpose(0, 2, 1)


def rows_of(blocks):
    return blocks.transpose(0, 2, 1).reshape(-1, blocks.shape[1])


MESH = pl.DeviceIdType.MESH
CHUNKS = 4


def place():
    user = lax.axis_index("user")
    return lax.div(user, 2), lax.rem(user, 2), lax.axis_index("item")


def plane():
    z, y, item = place()
    n = 2 * lax.axis_size("item")
    me = y * lax.axis_size("item") + item
    out = []
    for o in range(1, n):
        p = lax.rem(me + o, n)
        out.append({"user": 2 * z + lax.div(p, n // 2), "item": lax.rem(p, n // 2)})
    return n, me, out


def column():
    z, y, item = place()
    n = lax.axis_size("user") // 2
    return n, z, [{"user": 2 * lax.rem(z + o, n) + y, "item": item} for o in range(1, n)]


def facing():
    z, y, item = place()
    return {"user": 2 * z + 1 - y, "item": item}


def meet(devices):
    barrier = pltpu.get_barrier_semaphore()
    for device in devices:
        pl.semaphore_signal(barrier, inc=1, device_id=device, device_id_type=MESH)
    pl.semaphore_wait(barrier, len(devices))


def remote(src, dst, send, recv, device):
    return pltpu.make_async_remote_copy(
        src_ref=src, dst_ref=dst, send_sem=send, recv_sem=recv, device_id=device,
        device_id_type=MESH,
    )


def sum_over(group, value, slots, send, recv):
    n, me, devices = group
    slots[me] = value
    copies = [
        remote(slots.at[me], slots.at[me], send.at[o], recv.at[o], device)
        for o, device in enumerate(devices)
    ]
    for copy in copies:
        copy.start()
    for copy in copies:
        copy.wait()
    total = slots[0]
    for i in range(1, n):
        total = total + slots[i]
    return total


def gather_kernel(cat_ref, v_ref, stats_ref, slots_p, slots_c, sp, rp, sc, rc, sz, rz, sy, ry):
    nlock = stats_ref.shape[0]
    width = v_ref.shape[1]
    meet(plane()[2] + column()[2])
    lock = cat_ref[:nlock]
    stats = lax.dot_general(lock, cat_ref[...], NT, preferred_element_type=jnp.float32)
    stats = sum_over(plane(), stats, slots_p, sp, rp)
    stats = sum_over(column(), stats, slots_c, sc, rc)
    stats_ref[...] = stats
    projt = stats.T[nlock : nlock + width]
    own = cat_ref.shape[1] // TILE
    n, z, devices = column()
    y = place()[1]

    def block(o):
        at = (2 * lax.rem(z + n - o, n) + y) * own
        return v_ref.at[pl.ds(at, own)]

    for j in range(own):
        at = slice(j * TILE, (j + 1) * TILE)
        v = cat_ref[nlock : nlock + width, at].astype(jnp.float32)
        part = jnp.dot(projt, cat_ref[:nlock, at].astype(jnp.float32), precision=HIGH)
        v_ref[(2 * z + y) * own + j] = (v - part).astype(v_ref.dtype)
    down = [
        remote(block(0), block(0), sz.at[o], rz.at[o], device)
        for o, device in enumerate(devices)
    ]
    over = [remote(block(o), block(o), sy.at[o], ry.at[o], facing()) for o in range(n)]
    for copy in down:
        copy.start()
    over[0].start()
    for o in range(1, n):
        down[o - 1].wait_recv()
        over[o].start()
    for copy in down:
        copy.wait_send()
    for copy in over:
        copy.wait()


def user_sum_kernel(part_ref, u_ref, near, pair, far, sem):
    me = lax.axis_index("item")
    side = lax.rem(me, 2)
    sibling = {"item": me + 1 - 2 * side}
    across = {"item": lax.rem(me + 2, 4)}
    half = part_ref.shape[0] // 2
    size = half // CHUNKS
    meet([sibling, across])

    def copies(step, src, src_at, dst, dst_at, device):
        return [
            remote(
                src.at[pl.ds(src_at + k * size, size)],
                dst.at[pl.ds(dst_at + k * size, size)],
                sem.at[2 * step, k],
                sem.at[2 * step + 1, k],
                device,
            )
            for k in range(CHUNKS)
        ]

    give = copies(0, part_ref, (1 - side) * half, near, 0, sibling)
    swap = copies(1, pair, 0, far, 0, across)
    back = copies(2, u_ref, side * half, u_ref, side * half, sibling)
    for copy in give:
        copy.start()
    for k in range(CHUNKS):
        give[k].wait_recv()
        at = pl.ds(k * size, size)
        own = part_ref[pl.ds(side * half + k * size, size)].astype(jnp.float32)
        pair[at] = (own + near[at].astype(jnp.float32)).astype(pair.dtype)
        swap[k].start()
    for k in range(CHUNKS):
        swap[k].wait_recv()
        at = pl.ds(k * size, size)
        total = pair[at].astype(jnp.float32) + far[at].astype(jnp.float32)
        u_ref[pl.ds(side * half + k * size, size)] = total.astype(u_ref.dtype)
        back[k].start()
    for k in range(CHUNKS):
        give[k].wait_send()
        swap[k].wait_send()
        back[k].wait()


def finish_kernel(
    items, part_ref, lock_ref, stats_ref, v_ref,
    near, pair, land, slots_p, slots_c, sy, ry, sz, rz, sp, rp, sc, rc,
):
    nlock = stats_ref.shape[0]
    own, width, tile = land.shape[1:]
    n, z, devices = column()
    y = place()[1]
    meet(plane()[2] + devices)

    def piece(t, side):
        return pl.ds((2 * lax.rem(z + 1 + t, n) + side) * own, own)

    over = [
        remote(part_ref.at[piece(t, 1 - y)], near.at[t], sy.at[t], ry.at[t], facing())
        for t in range(n)
    ]
    down = [
        remote(pair.at[t], land.at[t], sz.at[t], rz.at[t], device)
        for t, device in enumerate(devices)
    ]
    for copy in over:
        copy.start()
    for t in range(n):
        over[t].wait_recv()
        both = part_ref[piece(t, y)].astype(jnp.float32) + near[t].astype(jnp.float32)
        if t < n - 1:
            pair[t] = both.astype(pair.dtype)
            down[t].start()
    for copy in over:
        copy.wait_send()
    for copy in down:
        copy.wait()
    back, square = [], jnp.zeros((width, tile), jnp.float32)
    rows = nlock + 8
    sums = jnp.zeros((rows, width), jnp.float32)
    for j in range(own):
        b = part_ref[(2 * z + y) * own + j].astype(jnp.float32) + near[n - 1, j].astype(
            jnp.float32
        )
        for t in range(n - 1):
            b = b + land[t, j].astype(jnp.float32)
        back.append(b)
        square = square + b * b
        lock = lock_ref[:rows, j * tile : (j + 1) * tile].astype(jnp.float32)
        sums = sums + lax.dot_general(
            lock, b, NT, precision=HIGH, preferred_element_type=jnp.float32
        )
    squares = lax.dot_general(
        jnp.ones((rows, tile), jnp.float32), square, NT, precision=HIGH,
        preferred_element_type=jnp.float32,
    )
    lane = lax.broadcasted_iota(jnp.int32, (rows, width), 0)
    sums = jnp.where(lane >= nlock, squares, sums)
    sums = jnp.concatenate([sums, jnp.zeros((rows, tile - width), jnp.float32)], axis=1)
    sums = sum_over(plane(), sums, slots_p, sp, rp)
    sums = sum_over(column(), sums, slots_c, sc, rc)
    sums = sums.T[:width]
    proj2, backsq = sums[:, :nlock], sums[:, nlock : nlock + 1]
    gram = stats_ref[:, :nlock]
    crossed = jnp.dot(proj2, gram, precision=HIGH) - 2.0 * proj2
    colsq = backsq + jnp.sum(proj2 * crossed, axis=1, keepdims=True)
    scale = 1.0 / jnp.sqrt(jnp.maximum(colsq, 0.0) / items + 1e-06)
    for j in range(own):
        lock = lock_ref[:nlock, j * tile : (j + 1) * tile].astype(jnp.float32)
        rest = back[j] - jnp.dot(proj2, lock, precision=HIGH)
        v_ref[j * tile : (j + 1) * tile, :] = (rest * scale).T


def comm_call(kernel, name, key, out_shape, scratch, *args):
    vmem = pl.BlockSpec(memory_space=pltpu.VMEM)
    return pl.pallas_call(
        kernel,
        name=name,
        out_shape=out_shape,
        in_specs=[vmem] * len(args),
        out_specs=jax.tree.map(lambda _: vmem, out_shape),
        scratch_shapes=scratch,
        compiler_params=pltpu.CompilerParams(
            collective_id=key, has_side_effects=True, vmem_limit_bytes=16 << 20
        ),
    )(*args)


def sems(*shape):
    return pltpu.SemaphoreType.DMA(shape)


def remote_plan(v_start, locked, tile_rows, tile_cols, tile_seeds, tile_count):
    n_user, n_item = lax.axis_size("user"), lax.axis_size("item")
    shard, width = v_start.shape
    nlock = locked.shape[1]
    nblocks = shard * n_user // TILE
    pad = jnp.zeros((shard, TILE - nlock - width), v_start.dtype)
    cat = jnp.concatenate([locked, v_start, pad], axis=1).T
    slab = (nblocks, width, TILE)
    wide, deep = 2 * n_item, n_user // 2
    pair = [sems(wide - 1)] * 2 + [sems(deep - 1)] * 2
    vblocks, stats = comm_call(
        gather_kernel,
        "gather",
        0,
        (
            jax.ShapeDtypeStruct(slab, jnp.bfloat16),
            jax.ShapeDtypeStruct((nlock, TILE), jnp.float32),
        ),
        [
            pltpu.VMEM((wide, nlock, TILE), jnp.float32),
            pltpu.VMEM((deep, nlock, TILE), jnp.float32),
        ]
        + pair
        + [sems(deep - 1)] * 2
        + [sems(deep)] * 2,
        cat,
    )
    tiles, upart = forward(tile_rows, tile_cols, tile_seeds, tile_count, vblocks, jnp.bfloat16)
    half = pltpu.VMEM((RB // 2, width, TILE), jnp.bfloat16)
    ublocks = comm_call(
        user_sum_kernel,
        "user_sum",
        1,
        jax.ShapeDtypeStruct((RB, width, TILE), jnp.bfloat16),
        [half, half, half, sems(6, CHUNKS)],
        upart,
    )
    wpart = backward(tile_rows, tile_cols, tile_count, ublocks, tiles, nblocks, jnp.bfloat16)
    per = RB // n_item
    u_factor = rows_of(lax.dynamic_slice_in_dim(ublocks, lax.axis_index("item") * per, per, 0))
    only = jnp.concatenate([locked, jnp.zeros((shard, TILE - nlock), locked.dtype)], axis=1).T
    v_next = comm_call(
        functools.partial(finish_kernel, float(shard * n_user * n_item)),
        "finish",
        2,
        jax.ShapeDtypeStruct((shard, width), jnp.float32),
        [
            pltpu.VMEM((deep, nblocks // n_user, width, TILE), jnp.bfloat16),
            pltpu.VMEM((deep - 1, nblocks // n_user, width, TILE), jnp.bfloat16),
            pltpu.VMEM((deep - 1, nblocks // n_user, width, TILE), jnp.bfloat16),
            pltpu.VMEM((wide, nlock + 8, TILE), jnp.float32),
            pltpu.VMEM((deep, nlock + 8, TILE), jnp.float32),
        ]
        + [sems(deep)] * 2
        + [sems(deep - 1)] * 2
        + pair,
        wpart,
        only,
        stats,
    )
    return (u_factor, v_next)


def on_device(v_start, locked, tile_rows, tile_cols, tile_seeds, tile_count):
    if v_start.shape[0] % TILE == 0 and lax.axis_size("item") == 4 and lax.axis_size("user") % 2 == 0:
        return remote_plan(v_start, locked, tile_rows, tile_cols, tile_seeds, tile_count)
    both = ("user", "item")
    lockf = locked.astype(jnp.float32)
    nlock = locked.shape[1]
    n_user, n_item = lax.axis_size("user"), lax.axis_size("item")
    slab = v_start.shape[0] * n_user
    stats = jnp.dot(
        locked.T, jnp.concatenate([v_start, locked], axis=1), preferred_element_type=jnp.float32
    )
    stats = lax.psum(stats, both)
    proj, gram = stats[:, :-nlock], stats[:, -nlock:]
    deflated = (v_start.astype(jnp.float32) - jnp.dot(lockf, proj, precision=HIGH)).astype(
        jnp.bfloat16
    )
    vslab = lax.all_gather(deflated, "user", axis=0, tiled=True)
    tiles, upart = forward(
        tile_rows, tile_cols, tile_seeds, tile_count, blocks_of(vslab), jnp.float32
    )
    ublocks = lax.psum(upart, "item").astype(jnp.bfloat16)
    per = RB // n_item
    u_factor = rows_of(lax.dynamic_slice_in_dim(ublocks, lax.axis_index("item") * per, per, 0))
    wpart = backward(
        tile_rows, tile_cols, tile_count, ublocks, tiles, slab // TILE, jnp.float32
    )
    back = lax.psum_scatter(rows_of(wpart), "user", scatter_dimension=0, tiled=True)
    sums = jnp.concatenate(
        [jnp.dot(lockf.T, back, precision=HIGH), jnp.sum(back * back, axis=0)[None]], axis=0
    )
    sums = lax.psum(sums, both)
    proj2, backsq = sums[:-1], sums[-1]
    rest = back - jnp.dot(lockf, proj2, precision=HIGH)
    crossed = jnp.dot(gram, proj2, precision=HIGH) - 2.0 * proj2
    colsq = jnp.maximum(backsq + jnp.sum(proj2 * crossed, axis=0), 0.0)
    v_next = rest / jnp.sqrt(colsq / (slab * n_item) + 1e-06)
    return (u_factor, v_next)


def solution(mesh):
    spec = P(("user", "item"), None)
    return jax.shard_map(
        on_device, mesh=mesh, in_specs=(spec,) * 6, out_specs=(spec, spec), check_vma=False
    )
```

```python
import functools

import jax
import jax.numpy as jnp
from jax import lax
from jax.experimental import pallas as pl
from jax.experimental.pallas import tpu as pltpu
from jax.sharding import PartitionSpec as P

TILE = 128
RB = 64
LIMIT = 16 << 20
GROUP = 16
SCALE = 1.0 / 1024.0
HIGH = lax.Precision.HIGHEST
NT = (((1,), (1,)), ((), ()))
NN = (((1,), (0,)), ((), ()))


def fill(seeds, tiles_ref, first, last):
    a = lax.broadcasted_iota(jnp.int32, (TILE, TILE), 0)
    b = lax.broadcasted_iota(jnp.int32, (TILE, TILE), 1)
    base = (a * TILE + b) * 40503

    def step(g, carry):
        for j in range(GROUP):
            s = g * GROUP + j
            h = base + seeds[0, s] * 9973
            h = h ^ (h >> 13)
            h = h * 1597334677
            h = h ^ (h >> 16)
            levels = ((h >> 8) & 255) - 128
            tiles_ref[s] = levels.astype(jnp.float32).astype(jnp.bfloat16)
        return carry

    lax.fori_loop(first, last, step, 0)


def fill_kernel(seeds, tiles_ref):
    fill(seeds, tiles_ref, 0, tiles_ref.shape[0] // GROUP)


def product_kernel(dims, forward, places, count, x_ref, tiles_ref, out_ref, acc):
    blocks = out_ref.shape[0]
    live = count[0, 0]
    acc[...] = jnp.zeros_like(acc)

    def step(g, carry):
        for j in range(GROUP):
            s = g * GROUP + j
            row, col = places[0, s] >> 16, places[0, s] & 65535
            source, target = (col, row) if forward else (row, col)
            target = jnp.where(s < live, target, blocks)
            acc[target] += lax.dot_general(
                x_ref[source], tiles_ref[s], dims, preferred_element_type=jnp.float32
            )
        return carry

    lax.fori_loop(0, lax.div(live + (GROUP - 1), GROUP), step, 0)
    out_ref[...] = (acc[:blocks] * SCALE).astype(out_ref.dtype)


VMEM_SPEC = pl.BlockSpec(memory_space=pltpu.VMEM)
SMEM_SPEC = pl.BlockSpec(memory_space=pltpu.SMEM)


def product(forward, places, count, x, tiles, nblocks, dtype):
    width, tile = x.shape[1:]
    return pl.pallas_call(
        functools.partial(product_kernel, NT if forward else NN, forward),
        name="forward" if forward else "backward",
        out_shape=jax.ShapeDtypeStruct((nblocks, width, tile), dtype),
        in_specs=[SMEM_SPEC, SMEM_SPEC, VMEM_SPEC, VMEM_SPEC],
        out_specs=VMEM_SPEC,
        scratch_shapes=[pltpu.VMEM((nblocks + 1, width, tile), jnp.float32)],
        compiler_params=pltpu.CompilerParams(vmem_limit_bytes=LIMIT),
    )(places, count, x, tiles)


def pack(tile_rows, tile_cols):
    return tile_rows * 65536 + tile_cols


def blocks_of(x):
    return x.reshape(-1, TILE, x.shape[1]).transpose(0, 2, 1)


def rows_of(blocks):
    return blocks.transpose(0, 2, 1).reshape(-1, blocks.shape[1])


MESH = pl.DeviceIdType.MESH
CHUNKS = 4


def place():
    user = lax.axis_index("user")
    return lax.div(user, 2), lax.rem(user, 2), lax.axis_index("item")


def plane():
    z, y, item = place()
    n = 2 * lax.axis_size("item")
    me = y * lax.axis_size("item") + item
    out = []
    for o in range(1, n):
        p = lax.rem(me + o, n)
        out.append({"user": 2 * z + lax.div(p, n // 2), "item": lax.rem(p, n // 2)})
    return n, me, out


def column():
    z, y, item = place()
    n = lax.axis_size("user") // 2
    return n, z, [{"user": 2 * lax.rem(z + o, n) + y, "item": item} for o in range(1, n)]


def facing():
    z, y, item = place()
    return {"user": 2 * z + 1 - y, "item": item}


def meet(devices):
    barrier = pltpu.get_barrier_semaphore()
    for device in devices:
        pl.semaphore_signal(barrier, inc=1, device_id=device, device_id_type=MESH)
    pl.semaphore_wait(barrier, len(devices))


def remote(src, dst, send, recv, device):
    return pltpu.make_async_remote_copy(
        src_ref=src, dst_ref=dst, send_sem=send, recv_sem=recv, device_id=device,
        device_id_type=MESH,
    )


def sum_over(group, value, slots, send, recv, meanwhile=lambda: None):
    n, me, devices = group
    slots[me] = value
    copies = [
        remote(slots.at[me], slots.at[me], send.at[o], recv.at[o], device)
        for o, device in enumerate(devices)
    ]
    for copy in copies:
        copy.start()
    meanwhile()
    for copy in copies:
        copy.wait()
    total = slots[0]
    for i in range(1, n):
        total = total + slots[i]
    return total


def gather_kernel(
    seeds, cat_ref, v_ref, stats_ref, tiles_ref,
    slots_p, slots_c, sp, rp, sc, rc, sz, rz, sy, ry,
):
    groups = tiles_ref.shape[0] // GROUP
    parts = 2 + lax.axis_size("user") // 2 - 1

    def some(i):
        fill(seeds, tiles_ref, groups * i // parts, groups * (i + 1) // parts)

    nlock = stats_ref.shape[0]
    width = v_ref.shape[1]
    meet(plane()[2] + column()[2])
    lock = cat_ref[:nlock]
    stats = lax.dot_general(lock, cat_ref[...], NT, preferred_element_type=jnp.float32)
    stats = sum_over(plane(), stats, slots_p, sp, rp, lambda: some(0))
    stats = sum_over(column(), stats, slots_c, sc, rc, lambda: some(1))
    stats_ref[...] = stats
    projt = stats.T[nlock : nlock + width]
    own = cat_ref.shape[1] // TILE
    n, z, devices = column()
    y = place()[1]

    def block(o):
        at = (2 * lax.rem(z + n - o, n) + y) * own
        return v_ref.at[pl.ds(at, own)]

    for j in range(own):
        at = slice(j * TILE, (j + 1) * TILE)
        v = cat_ref[nlock : nlock + width, at].astype(jnp.float32)
        part = jnp.dot(projt, cat_ref[:nlock, at].astype(jnp.float32), precision=HIGH)
        v_ref[(2 * z + y) * own + j] = (v - part).astype(v_ref.dtype)
    down = [
        remote(block(0), block(0), sz.at[o], rz.at[o], device)
        for o, device in enumerate(devices)
    ]
    over = [remote(block(o), block(o), sy.at[o], ry.at[o], facing()) for o in range(n)]
    for copy in down:
        copy.start()
    over[0].start()
    for o in range(1, n):
        some(1 + o)
        down[o - 1].wait_recv()
        over[o].start()
    for copy in down:
        copy.wait_send()
    for copy in over:
        copy.wait()


def user_sum_kernel(part_ref, u_ref, near, pair, far, sem):
    me = lax.axis_index("item")
    side = lax.rem(me, 2)
    sibling = {"item": me + 1 - 2 * side}
    across = {"item": lax.rem(me + 2, 4)}
    half = part_ref.shape[0] // 2
    size = half // CHUNKS
    meet([sibling, across])

    def copies(step, src, src_at, dst, dst_at, device):
        return [
            remote(
                src.at[pl.ds(src_at + k * size, size)],
                dst.at[pl.ds(dst_at + k * size, size)],
                sem.at[2 * step, k],
                sem.at[2 * step + 1, k],
                device,
            )
            for k in range(CHUNKS)
        ]

    give = copies(0, part_ref, (1 - side) * half, near, 0, sibling)
    swap = copies(1, pair, 0, far, 0, across)
    back = copies(2, u_ref, side * half, u_ref, side * half, sibling)
    for copy in give:
        copy.start()
    for k in range(CHUNKS):
        give[k].wait_recv()
        at = pl.ds(k * size, size)
        own = part_ref[pl.ds(side * half + k * size, size)].astype(jnp.float32)
        pair[at] = (own + near[at].astype(jnp.float32)).astype(pair.dtype)
        swap[k].start()
    for k in range(CHUNKS):
        swap[k].wait_recv()
        at = pl.ds(k * size, size)
        total = pair[at].astype(jnp.float32) + far[at].astype(jnp.float32)
        u_ref[pl.ds(side * half + k * size, size)] = total.astype(u_ref.dtype)
        back[k].start()
    for k in range(CHUNKS):
        give[k].wait_send()
        swap[k].wait_send()
        back[k].wait()


def finish_kernel(
    items, part_ref, lock_ref, stats_ref, v_ref,
    near, pair, land, slots_p, slots_c, sy, ry, sz, rz, sp, rp, sc, rc,
):
    nlock = stats_ref.shape[0]
    own, width, tile = land.shape[1:]
    n, z, devices = column()
    y = place()[1]
    meet(plane()[2] + devices)

    def piece(t, side):
        return pl.ds((2 * lax.rem(z + 1 + t, n) + side) * own, own)

    over = [
        remote(part_ref.at[piece(t, 1 - y)], near.at[t], sy.at[t], ry.at[t], facing())
        for t in range(n)
    ]
    down = [
        remote(pair.at[t], land.at[t], sz.at[t], rz.at[t], device)
        for t, device in enumerate(devices)
    ]
    for copy in over:
        copy.start()
    for t in range(n):
        over[t].wait_recv()
        both = part_ref[piece(t, y)].astype(jnp.float32) + near[t].astype(jnp.float32)
        if t < n - 1:
            pair[t] = both.astype(pair.dtype)
            down[t].start()
    for copy in over:
        copy.wait_send()
    for copy in down:
        copy.wait()
    back, square = [], jnp.zeros((width, tile), jnp.float32)
    rows = nlock + 8
    sums = jnp.zeros((rows, width), jnp.float32)
    for j in range(own):
        b = part_ref[(2 * z + y) * own + j].astype(jnp.float32) + near[n - 1, j].astype(
            jnp.float32
        )
        for t in range(n - 1):
            b = b + land[t, j].astype(jnp.float32)
        back.append(b)
        square = square + b * b
        lock = lock_ref[:rows, j * tile : (j + 1) * tile].astype(jnp.float32)
        sums = sums + lax.dot_general(
            lock, b, NT, precision=HIGH, preferred_element_type=jnp.float32
        )
    squares = lax.dot_general(
        jnp.ones((rows, tile), jnp.float32), square, NT, precision=HIGH,
        preferred_element_type=jnp.float32,
    )
    lane = lax.broadcasted_iota(jnp.int32, (rows, width), 0)
    sums = jnp.where(lane >= nlock, squares, sums)
    sums = jnp.concatenate([sums, jnp.zeros((rows, tile - width), jnp.float32)], axis=1)
    sums = sum_over(plane(), sums, slots_p, sp, rp)
    sums = sum_over(column(), sums, slots_c, sc, rc)
    sums = sums.T[:width]
    proj2, backsq = sums[:, :nlock], sums[:, nlock : nlock + 1]
    gram = stats_ref[:, :nlock]
    crossed = jnp.dot(proj2, gram, precision=HIGH) - 2.0 * proj2
    colsq = backsq + jnp.sum(proj2 * crossed, axis=1, keepdims=True)
    scale = 1.0 / jnp.sqrt(jnp.maximum(colsq, 0.0) / items + 1e-06)
    for j in range(own):
        lock = lock_ref[:nlock, j * tile : (j + 1) * tile].astype(jnp.float32)
        rest = back[j] - jnp.dot(proj2, lock, precision=HIGH)
        v_ref[j * tile : (j + 1) * tile, :] = (rest * scale).T


def comm_call(kernel, name, key, out_shape, scratch, *args):
    vmem = pl.BlockSpec(memory_space=pltpu.VMEM)
    return pl.pallas_call(
        kernel,
        name=name,
        out_shape=out_shape,
        in_specs=[SMEM_SPEC if x.dtype == jnp.int32 else vmem for x in args],
        out_specs=jax.tree.map(lambda _: vmem, out_shape),
        scratch_shapes=scratch,
        compiler_params=pltpu.CompilerParams(
            collective_id=key, has_side_effects=True, vmem_limit_bytes=LIMIT
        ),
    )(*args)


def sems(*shape):
    return pltpu.SemaphoreType.DMA(shape)


def remote_plan(v_start, locked, tile_rows, tile_cols, tile_seeds, tile_count):
    n_user, n_item = lax.axis_size("user"), lax.axis_size("item")
    shard, width = v_start.shape
    nlock = locked.shape[1]
    nblocks = shard * n_user // TILE
    pad = jnp.zeros((shard, TILE - nlock - width), v_start.dtype)
    cat = jnp.concatenate([locked, v_start, pad], axis=1).T
    slab = (nblocks, width, TILE)
    wide, deep = 2 * n_item, n_user // 2
    pair = [sems(wide - 1)] * 2 + [sems(deep - 1)] * 2
    vblocks, stats, tiles = comm_call(
        gather_kernel,
        "gather",
        0,
        (
            jax.ShapeDtypeStruct(slab, jnp.bfloat16),
            jax.ShapeDtypeStruct((nlock, TILE), jnp.float32),
            jax.ShapeDtypeStruct((tile_seeds.shape[1], TILE, TILE), jnp.bfloat16),
        ),
        [
            pltpu.VMEM((wide, nlock, TILE), jnp.float32),
            pltpu.VMEM((deep, nlock, TILE), jnp.float32),
        ]
        + pair
        + [sems(deep - 1)] * 2
        + [sems(deep)] * 2,
        tile_seeds,
        cat,
    )
    places = pack(tile_rows, tile_cols)
    upart = product(True, places, tile_count, vblocks, tiles, RB, jnp.bfloat16)
    half = pltpu.VMEM((RB // 2, width, TILE), jnp.bfloat16)
    ublocks = comm_call(
        user_sum_kernel,
        "user_sum",
        1,
        jax.ShapeDtypeStruct((RB, width, TILE), jnp.bfloat16),
        [half, half, half, sems(6, CHUNKS)],
        upart,
    )
    wpart = product(False, places, tile_count, ublocks, tiles, nblocks, jnp.bfloat16)
    per = RB // n_item
    u_factor = rows_of(lax.dynamic_slice_in_dim(ublocks, lax.axis_index("item") * per, per, 0))
    only = jnp.concatenate([locked, jnp.zeros((shard, TILE - nlock), locked.dtype)], axis=1).T
    v_next = comm_call(
        functools.partial(finish_kernel, float(shard * n_user * n_item)),
        "finish",
        2,
        jax.ShapeDtypeStruct((shard, width), jnp.float32),
        [
            pltpu.VMEM((deep, nblocks // n_user, width, TILE), jnp.bfloat16),
            pltpu.VMEM((deep - 1, nblocks // n_user, width, TILE), jnp.bfloat16),
            pltpu.VMEM((deep - 1, nblocks // n_user, width, TILE), jnp.bfloat16),
            pltpu.VMEM((wide, nlock + 8, TILE), jnp.float32),
            pltpu.VMEM((deep, nlock + 8, TILE), jnp.float32),
        ]
        + [sems(deep)] * 2
        + [sems(deep - 1)] * 2
        + pair,
        wpart,
        only,
        stats,
    )
    return (u_factor, v_next)


def on_device(v_start, locked, tile_rows, tile_cols, tile_seeds, tile_count):
    if v_start.shape[0] % TILE == 0 and lax.axis_size("item") == 4 and lax.axis_size("user") % 2 == 0:
        return remote_plan(v_start, locked, tile_rows, tile_cols, tile_seeds, tile_count)
    both = ("user", "item")
    lockf = locked.astype(jnp.float32)
    nlock = locked.shape[1]
    n_user, n_item = lax.axis_size("user"), lax.axis_size("item")
    slab = v_start.shape[0] * n_user
    stats = jnp.dot(
        locked.T, jnp.concatenate([v_start, locked], axis=1), preferred_element_type=jnp.float32
    )
    stats = lax.psum(stats, both)
    proj, gram = stats[:, :-nlock], stats[:, -nlock:]
    deflated = (v_start.astype(jnp.float32) - jnp.dot(lockf, proj, precision=HIGH)).astype(
        jnp.bfloat16
    )
    vslab = lax.all_gather(deflated, "user", axis=0, tiled=True)
    places = pack(tile_rows, tile_cols)
    tiles = pl.pallas_call(
        fill_kernel,
        name="fill",
        out_shape=jax.ShapeDtypeStruct((tile_seeds.shape[1], TILE, TILE), jnp.bfloat16),
        in_specs=[SMEM_SPEC],
        out_specs=VMEM_SPEC,
        compiler_params=pltpu.CompilerParams(vmem_limit_bytes=LIMIT),
    )(tile_seeds)
    upart = product(True, places, tile_count, blocks_of(vslab), tiles, RB, jnp.float32)
    ublocks = lax.psum(upart, "item").astype(jnp.bfloat16)
    per = RB // n_item
    u_factor = rows_of(lax.dynamic_slice_in_dim(ublocks, lax.axis_index("item") * per, per, 0))
    wpart = product(False, places, tile_count, ublocks, tiles, slab // TILE, jnp.float32)
    back = lax.psum_scatter(rows_of(wpart), "user", scatter_dimension=0, tiled=True)
    sums = jnp.concatenate(
        [jnp.dot(lockf.T, back, precision=HIGH), jnp.sum(back * back, axis=0)[None]], axis=0
    )
    sums = lax.psum(sums, both)
    proj2, backsq = sums[:-1], sums[-1]
    rest = back - jnp.dot(lockf, proj2, precision=HIGH)
    crossed = jnp.dot(gram, proj2, precision=HIGH) - 2.0 * proj2
    colsq = jnp.maximum(backsq + jnp.sum(proj2 * crossed, axis=0), 0.0)
    v_next = rest / jnp.sqrt(colsq / (slab * n_item) + 1e-06)
    return (u_factor, v_next)


def solution(mesh):
    spec = P(("user", "item"), None)
    return jax.shard_map(
        on_device, mesh=mesh, in_specs=(spec,) * 6, out_specs=(spec, spec), check_vma=False
    )
```

```python
import functools

import jax
import jax.numpy as jnp
from jax import lax
from jax.experimental import pallas as pl
from jax.experimental.pallas import tpu as pltpu
from jax.sharding import PartitionSpec as P

TILE = 128
RB = 64
LIMIT = 16 << 20
GROUP = 16
SPAN = 32
SCALE = 1.0 / 1024.0
HIGH = lax.Precision.HIGHEST
NT = (((1,), (1,)), ((), ()))
NN = (((1,), (0,)), ((), ()))


def fill(seeds, tiles_ref, first, last, flip):
    a = lax.broadcasted_iota(jnp.int32, (TILE, TILE), 0)
    b = lax.broadcasted_iota(jnp.int32, (TILE, TILE), 1)
    base = (b * TILE + a if flip else a * TILE + b) * 40503

    def step(g, carry):
        for j in range(GROUP):
            s = g * GROUP + j
            h = base + seeds[0, s] * 9973
            h = h ^ (h >> 13)
            h = h * 1597334677
            h = h ^ (h >> 16)
            levels = ((h >> 8) & 255) - 128
            tiles_ref[s] = levels.astype(jnp.float32).astype(jnp.bfloat16)
        return carry

    lax.fori_loop(first, last, step, 0)


def fill_kernel(flip, seeds, tiles_ref):
    fill(seeds, tiles_ref, 0, tiles_ref.shape[0] // GROUP, flip)


def product_kernel(forward, places, count, x_ref, tiles_ref, out_ref, acc):
    blocks = out_ref.shape[0]
    live = count[0, 0]
    acc[...] = jnp.zeros_like(acc)

    def step(g, carry):
        for j in range(SPAN):
            s = g * SPAN + j
            row, col = places[0, s] >> 16, places[0, s] & 65535
            source, target = (col, row) if forward else (row, col)
            target = jnp.where(s < live, target, blocks)
            acc[target] += lax.dot_general(
                x_ref[source], tiles_ref[s], NN, preferred_element_type=jnp.float32
            )
        return carry

    lax.fori_loop(0, lax.div(live + (SPAN - 1), SPAN), step, 0)
    out_ref[...] = (acc[:blocks] * SCALE).astype(out_ref.dtype)


VMEM_SPEC = pl.BlockSpec(memory_space=pltpu.VMEM)
SMEM_SPEC = pl.BlockSpec(memory_space=pltpu.SMEM)


def product(forward, places, count, x, tiles, nblocks, dtype):
    width, tile = x.shape[1:]
    return pl.pallas_call(
        functools.partial(product_kernel, forward),
        name="forward" if forward else "backward",
        out_shape=jax.ShapeDtypeStruct((nblocks, width, tile), dtype),
        in_specs=[SMEM_SPEC, SMEM_SPEC, VMEM_SPEC, VMEM_SPEC],
        out_specs=VMEM_SPEC,
        scratch_shapes=[pltpu.VMEM((nblocks + 1, width, tile), jnp.float32)],
        compiler_params=pltpu.CompilerParams(vmem_limit_bytes=LIMIT),
    )(places, count, x, tiles)


def pack(tile_rows, tile_cols):
    return tile_rows * 65536 + tile_cols


def blocks_of(x):
    return x.reshape(-1, TILE, x.shape[1]).transpose(0, 2, 1)


def rows_of(blocks):
    return blocks.transpose(0, 2, 1).reshape(-1, blocks.shape[1])


MESH = pl.DeviceIdType.MESH
CHUNKS = 4


def place():
    user = lax.axis_index("user")
    return lax.div(user, 2), lax.rem(user, 2), lax.axis_index("item")


def plane():
    z, y, item = place()
    n = 2 * lax.axis_size("item")
    me = y * lax.axis_size("item") + item
    out = []
    for o in range(1, n):
        p = lax.rem(me + o, n)
        out.append({"user": 2 * z + lax.div(p, n // 2), "item": lax.rem(p, n // 2)})
    return n, me, out


def column():
    z, y, item = place()
    n = lax.axis_size("user") // 2
    return n, z, [{"user": 2 * lax.rem(z + o, n) + y, "item": item} for o in range(1, n)]


def facing():
    z, y, item = place()
    return {"user": 2 * z + 1 - y, "item": item}


def meet(devices):
    barrier = pltpu.get_barrier_semaphore()
    for device in devices:
        pl.semaphore_signal(barrier, inc=1, device_id=device, device_id_type=MESH)
    pl.semaphore_wait(barrier, len(devices))


def remote(src, dst, send, recv, device):
    return pltpu.make_async_remote_copy(
        src_ref=src, dst_ref=dst, send_sem=send, recv_sem=recv, device_id=device,
        device_id_type=MESH,
    )


def sum_over(group, value, slots, send, recv, meanwhile=lambda: None):
    n, me, devices = group
    slots[me] = value
    copies = [
        remote(slots.at[me], slots.at[me], send.at[o], recv.at[o], device)
        for o, device in enumerate(devices)
    ]
    for copy in copies:
        copy.start()
    meanwhile()
    for copy in copies:
        copy.wait()
    total = slots[0]
    for i in range(1, n):
        total = total + slots[i]
    return total


def gather_kernel(
    seeds, cat_ref, v_ref, stats_ref, tiles_ref,
    slots_p, slots_c, sp, rp, sc, rc, sz, rz, sy, ry,
):
    groups = tiles_ref.shape[0] // GROUP
    parts = 2 + lax.axis_size("user") // 2 - 1

    def some(i):
        fill(seeds, tiles_ref, groups * i // parts, groups * (i + 1) // parts, True)

    nlock = stats_ref.shape[0]
    width = v_ref.shape[1]
    meet(plane()[2] + column()[2])
    lock = cat_ref[:nlock]
    stats = lax.dot_general(lock, cat_ref[...], NT, preferred_element_type=jnp.float32)
    stats = sum_over(plane(), stats, slots_p, sp, rp, lambda: some(0))
    stats = sum_over(column(), stats, slots_c, sc, rc, lambda: some(1))
    stats_ref[...] = stats
    projt = stats.T[nlock : nlock + width]
    own = cat_ref.shape[1] // TILE
    n, z, devices = column()
    y = place()[1]

    def block(o):
        at = (2 * lax.rem(z + n - o, n) + y) * own
        return v_ref.at[pl.ds(at, own)]

    for j in range(own):
        at = slice(j * TILE, (j + 1) * TILE)
        v = cat_ref[nlock : nlock + width, at].astype(jnp.float32)
        part = jnp.dot(projt, cat_ref[:nlock, at].astype(jnp.float32), precision=HIGH)
        v_ref[(2 * z + y) * own + j] = (v - part).astype(v_ref.dtype)
    down = [
        remote(block(0), block(0), sz.at[o], rz.at[o], device)
        for o, device in enumerate(devices)
    ]
    over = [remote(block(o), block(o), sy.at[o], ry.at[o], facing()) for o in range(n)]
    for copy in down:
        copy.start()
    over[0].start()
    for o in range(1, n):
        some(1 + o)
        down[o - 1].wait_recv()
        over[o].start()
    for copy in down:
        copy.wait_send()
    for copy in over:
        copy.wait()


def user_sum_kernel(seeds, part_ref, u_ref, tiles_ref, near, pair, far, sem):
    groups = tiles_ref.shape[0] // GROUP
    early, late = groups // 32, groups * 6 // 32
    me = lax.axis_index("item")
    side = lax.rem(me, 2)
    sibling = {"item": me + 1 - 2 * side}
    across = {"item": lax.rem(me + 2, 4)}
    half = part_ref.shape[0] // 2
    size = half // CHUNKS
    meet([sibling, across])

    def copies(step, src, src_at, dst, dst_at, device):
        return [
            remote(
                src.at[pl.ds(src_at + k * size, size)],
                dst.at[pl.ds(dst_at + k * size, size)],
                sem.at[2 * step, k],
                sem.at[2 * step + 1, k],
                device,
            )
            for k in range(CHUNKS)
        ]

    give = copies(0, part_ref, (1 - side) * half, near, 0, sibling)
    swap = copies(1, pair, 0, far, 0, across)
    back = copies(2, u_ref, side * half, u_ref, side * half, sibling)
    for copy in give:
        copy.start()
    for k in range(CHUNKS):
        give[k].wait_recv()
        at = pl.ds(k * size, size)
        own = part_ref[pl.ds(side * half + k * size, size)].astype(jnp.float32)
        pair[at] = (own + near[at].astype(jnp.float32)).astype(pair.dtype)
        swap[k].start()
        fill(seeds, tiles_ref, k * early, (k + 1) * early, False)
    for k in range(CHUNKS):
        first = CHUNKS * early + k * late
        fill(seeds, tiles_ref, first, first + late, False)
        swap[k].wait_recv()
        at = pl.ds(k * size, size)
        total = pair[at].astype(jnp.float32) + far[at].astype(jnp.float32)
        u_ref[pl.ds(side * half + k * size, size)] = total.astype(u_ref.dtype)
        back[k].start()
    fill(seeds, tiles_ref, CHUNKS * (early + late), groups, False)
    for k in range(CHUNKS):
        give[k].wait_send()
        swap[k].wait_send()
        back[k].wait()


def finish_kernel(
    items, part_ref, lock_ref, stats_ref, v_ref,
    near, pair, land, slots_p, slots_c, sy, ry, sz, rz, sp, rp, sc, rc,
):
    nlock = stats_ref.shape[0]
    own, width, tile = land.shape[1:]
    n, z, devices = column()
    y = place()[1]
    meet(plane()[2] + devices)

    def piece(t, side):
        return pl.ds((2 * lax.rem(z + 1 + t, n) + side) * own, own)

    over = [
        remote(part_ref.at[piece(t, 1 - y)], near.at[t], sy.at[t], ry.at[t], facing())
        for t in range(n)
    ]
    down = [
        remote(pair.at[t], land.at[t], sz.at[t], rz.at[t], device)
        for t, device in enumerate(devices)
    ]
    for copy in over:
        copy.start()
    for t in range(n):
        over[t].wait_recv()
        both = part_ref[piece(t, y)].astype(jnp.float32) + near[t].astype(jnp.float32)
        if t < n - 1:
            pair[t] = both.astype(pair.dtype)
            down[t].start()
    for copy in over:
        copy.wait_send()
    for copy in down:
        copy.wait()
    back, square = [], jnp.zeros((width, tile), jnp.float32)
    rows = nlock + 8
    sums = jnp.zeros((rows, width), jnp.float32)
    for j in range(own):
        b = part_ref[(2 * z + y) * own + j].astype(jnp.float32) + near[n - 1, j].astype(
            jnp.float32
        )
        for t in range(n - 1):
            b = b + land[t, j].astype(jnp.float32)
        back.append(b)
        square = square + b * b
        lock = lock_ref[:rows, j * tile : (j + 1) * tile].astype(jnp.float32)
        sums = sums + lax.dot_general(
            lock, b, NT, precision=HIGH, preferred_element_type=jnp.float32
        )
    squares = lax.dot_general(
        jnp.ones((rows, tile), jnp.float32), square, NT, precision=HIGH,
        preferred_element_type=jnp.float32,
    )
    lane = lax.broadcasted_iota(jnp.int32, (rows, width), 0)
    sums = jnp.where(lane >= nlock, squares, sums)
    sums = jnp.concatenate([sums, jnp.zeros((rows, tile - width), jnp.float32)], axis=1)
    sums = sum_over(plane(), sums, slots_p, sp, rp)
    sums = sum_over(column(), sums, slots_c, sc, rc)
    sums = sums.T[:width]
    proj2, backsq = sums[:, :nlock], sums[:, nlock : nlock + 1]
    gram = stats_ref[:, :nlock]
    crossed = jnp.dot(proj2, gram, precision=HIGH) - 2.0 * proj2
    colsq = backsq + jnp.sum(proj2 * crossed, axis=1, keepdims=True)
    scale = 1.0 / jnp.sqrt(jnp.maximum(colsq, 0.0) / items + 1e-06)
    for j in range(own):
        lock = lock_ref[:nlock, j * tile : (j + 1) * tile].astype(jnp.float32)
        rest = back[j] - jnp.dot(proj2, lock, precision=HIGH)
        v_ref[j * tile : (j + 1) * tile, :] = (rest * scale).T


def comm_call(kernel, name, key, out_shape, scratch, *args):
    vmem = pl.BlockSpec(memory_space=pltpu.VMEM)
    return pl.pallas_call(
        kernel,
        name=name,
        out_shape=out_shape,
        in_specs=[SMEM_SPEC if x.dtype == jnp.int32 else vmem for x in args],
        out_specs=jax.tree.map(lambda _: vmem, out_shape),
        scratch_shapes=scratch,
        compiler_params=pltpu.CompilerParams(
            collective_id=key, has_side_effects=True, vmem_limit_bytes=LIMIT
        ),
    )(*args)


def sems(*shape):
    return pltpu.SemaphoreType.DMA(shape)


def remote_plan(v_start, locked, tile_rows, tile_cols, tile_seeds, tile_count):
    n_user, n_item = lax.axis_size("user"), lax.axis_size("item")
    shard, width = v_start.shape
    nlock = locked.shape[1]
    nblocks = shard * n_user // TILE
    pad = jnp.zeros((shard, TILE - nlock - width), v_start.dtype)
    cat = jnp.concatenate([locked, v_start, pad], axis=1).T
    slab = (nblocks, width, TILE)
    wide, deep = 2 * n_item, n_user // 2
    pair = [sems(wide - 1)] * 2 + [sems(deep - 1)] * 2
    vblocks, stats, tiles = comm_call(
        gather_kernel,
        "gather",
        0,
        (
            jax.ShapeDtypeStruct(slab, jnp.bfloat16),
            jax.ShapeDtypeStruct((nlock, TILE), jnp.float32),
            jax.ShapeDtypeStruct((tile_seeds.shape[1], TILE, TILE), jnp.bfloat16),
        ),
        [
            pltpu.VMEM((wide, nlock, TILE), jnp.float32),
            pltpu.VMEM((deep, nlock, TILE), jnp.float32),
        ]
        + pair
        + [sems(deep - 1)] * 2
        + [sems(deep)] * 2,
        tile_seeds,
        cat,
    )
    places = pack(tile_rows, tile_cols)
    upart = product(True, places, tile_count, vblocks, tiles, RB, jnp.bfloat16)
    half = pltpu.VMEM((RB // 2, width, TILE), jnp.bfloat16)
    ublocks, tiles = comm_call(
        user_sum_kernel,
        "user_sum",
        1,
        (
            jax.ShapeDtypeStruct((RB, width, TILE), jnp.bfloat16),
            jax.ShapeDtypeStruct((tile_seeds.shape[1], TILE, TILE), jnp.bfloat16),
        ),
        [half, half, half, sems(6, CHUNKS)],
        tile_seeds,
        upart,
    )
    wpart = product(False, places, tile_count, ublocks, tiles, nblocks, jnp.bfloat16)
    per = RB // n_item
    u_factor = rows_of(lax.dynamic_slice_in_dim(ublocks, lax.axis_index("item") * per, per, 0))
    only = jnp.concatenate([locked, jnp.zeros((shard, TILE - nlock), locked.dtype)], axis=1).T
    v_next = comm_call(
        functools.partial(finish_kernel, float(shard * n_user * n_item)),
        "finish",
        2,
        jax.ShapeDtypeStruct((shard, width), jnp.float32),
        [
            pltpu.VMEM((deep, nblocks // n_user, width, TILE), jnp.bfloat16),
            pltpu.VMEM((deep - 1, nblocks // n_user, width, TILE), jnp.bfloat16),
            pltpu.VMEM((deep - 1, nblocks // n_user, width, TILE), jnp.bfloat16),
            pltpu.VMEM((wide, nlock + 8, TILE), jnp.float32),
            pltpu.VMEM((deep, nlock + 8, TILE), jnp.float32),
        ]
        + [sems(deep)] * 2
        + [sems(deep - 1)] * 2
        + pair,
        wpart,
        only,
        stats,
    )
    return (u_factor, v_next)


def on_device(v_start, locked, tile_rows, tile_cols, tile_seeds, tile_count):
    if v_start.shape[0] % TILE == 0 and lax.axis_size("item") == 4 and lax.axis_size("user") % 2 == 0:
        return remote_plan(v_start, locked, tile_rows, tile_cols, tile_seeds, tile_count)
    both = ("user", "item")
    lockf = locked.astype(jnp.float32)
    nlock = locked.shape[1]
    n_user, n_item = lax.axis_size("user"), lax.axis_size("item")
    slab = v_start.shape[0] * n_user
    stats = jnp.dot(
        locked.T, jnp.concatenate([v_start, locked], axis=1), preferred_element_type=jnp.float32
    )
    stats = lax.psum(stats, both)
    proj, gram = stats[:, :-nlock], stats[:, -nlock:]
    deflated = (v_start.astype(jnp.float32) - jnp.dot(lockf, proj, precision=HIGH)).astype(
        jnp.bfloat16
    )
    vslab = lax.all_gather(deflated, "user", axis=0, tiled=True)
    places = pack(tile_rows, tile_cols)
    flipped, tiles = [
        pl.pallas_call(
            functools.partial(fill_kernel, flip),
            name="fill",
            out_shape=jax.ShapeDtypeStruct((tile_seeds.shape[1], TILE, TILE), jnp.bfloat16),
            in_specs=[SMEM_SPEC],
            out_specs=VMEM_SPEC,
            compiler_params=pltpu.CompilerParams(vmem_limit_bytes=LIMIT),
        )(tile_seeds)
        for flip in (True, False)
    ]
    upart = product(True, places, tile_count, blocks_of(vslab), flipped, RB, jnp.float32)
    ublocks = lax.psum(upart, "item").astype(jnp.bfloat16)
    per = RB // n_item
    u_factor = rows_of(lax.dynamic_slice_in_dim(ublocks, lax.axis_index("item") * per, per, 0))
    wpart = product(False, places, tile_count, ublocks, tiles, slab // TILE, jnp.float32)
    back = lax.psum_scatter(rows_of(wpart), "user", scatter_dimension=0, tiled=True)
    sums = jnp.concatenate(
        [jnp.dot(lockf.T, back, precision=HIGH), jnp.sum(back * back, axis=0)[None]], axis=0
    )
    sums = lax.psum(sums, both)
    proj2, backsq = sums[:-1], sums[-1]
    rest = back - jnp.dot(lockf, proj2, precision=HIGH)
    crossed = jnp.dot(gram, proj2, precision=HIGH) - 2.0 * proj2
    colsq = jnp.maximum(backsq + jnp.sum(proj2 * crossed, axis=0), 0.0)
    v_next = rest / jnp.sqrt(colsq / (slab * n_item) + 1e-06)
    return (u_factor, v_next)


def solution(mesh):
    spec = P(("user", "item"), None)
    return jax.shard_map(
        on_device, mesh=mesh, in_specs=(spec,) * 6, out_specs=(spec, spec), check_vma=False
    )
```

```python
import functools

import jax
import jax.numpy as jnp
from jax import lax
from jax.experimental import pallas as pl
from jax.experimental.pallas import tpu as pltpu
from jax.sharding import PartitionSpec as P

TILE = 128
RB = 64
LIMIT = 16 << 20
GROUP = 16
SPAN = 64
SCALE = 1.0 / 1024.0
HIGH = lax.Precision.HIGHEST
NT = (((1,), (1,)), ((), ()))
NN = (((1,), (0,)), ((), ()))


def fill(seeds, tiles_ref, first, last, flip):
    a = lax.broadcasted_iota(jnp.int32, (TILE, TILE), 0)
    b = lax.broadcasted_iota(jnp.int32, (TILE, TILE), 1)
    base = (b * TILE + a if flip else a * TILE + b) * 40503

    def step(g, carry):
        for j in range(GROUP):
            s = g * GROUP + j
            h = base + seeds[0, s] * 9973
            h = h ^ (h >> 13)
            h = h * 1597334677
            h = h ^ (h >> 16)
            levels = ((h >> 8) & 255) - 128
            tiles_ref[s] = levels.astype(jnp.float32).astype(jnp.bfloat16)
        return carry

    lax.fori_loop(first, last, step, 0)


def fill_kernel(flip, seeds, tiles_ref):
    fill(seeds, tiles_ref, 0, tiles_ref.shape[0] // GROUP, flip)


def product_kernel(forward, places, count, x_ref, tiles_ref, out_ref, acc):
    blocks = out_ref.shape[0]
    live = count[0, 0]
    acc[...] = jnp.zeros_like(acc)

    def step(g, carry):
        for j in range(SPAN):
            s = g * SPAN + j
            row, col = places[0, s] >> 16, places[0, s] & 65535
            source, target = (col, row) if forward else (row, col)
            target = jnp.where(s < live, target, blocks)
            acc[target] += lax.dot_general(
                x_ref[source], tiles_ref[s], NN, preferred_element_type=jnp.float32
            )
        return carry

    lax.fori_loop(0, lax.div(live + (SPAN - 1), SPAN), step, 0)
    out_ref[...] = (acc[:blocks] * SCALE).astype(out_ref.dtype)


VMEM_SPEC = pl.BlockSpec(memory_space=pltpu.VMEM)
SMEM_SPEC = pl.BlockSpec(memory_space=pltpu.SMEM)


def product(forward, places, count, x, tiles, nblocks, dtype):
    width, tile = x.shape[1:]
    return pl.pallas_call(
        functools.partial(product_kernel, forward),
        name="forward" if forward else "backward",
        out_shape=jax.ShapeDtypeStruct((nblocks, width, tile), dtype),
        in_specs=[SMEM_SPEC, SMEM_SPEC, VMEM_SPEC, VMEM_SPEC],
        out_specs=VMEM_SPEC,
        scratch_shapes=[pltpu.VMEM((nblocks + 1, width, tile), jnp.float32)],
        compiler_params=pltpu.CompilerParams(vmem_limit_bytes=LIMIT),
    )(places, count, x, tiles)


def pack(tile_rows, tile_cols):
    return tile_rows * 65536 + tile_cols


def blocks_of(x):
    return x.reshape(-1, TILE, x.shape[1]).transpose(0, 2, 1)


def rows_of(blocks):
    return blocks.transpose(0, 2, 1).reshape(-1, blocks.shape[1])


MESH = pl.DeviceIdType.MESH
CHUNKS = 4


def place():
    user = lax.axis_index("user")
    return lax.div(user, 2), lax.rem(user, 2), lax.axis_index("item")


def plane():
    z, y, item = place()
    n = 2 * lax.axis_size("item")
    me = y * lax.axis_size("item") + item
    out = []
    for o in range(1, n):
        p = lax.rem(me + o, n)
        out.append({"user": 2 * z + lax.div(p, n // 2), "item": lax.rem(p, n // 2)})
    return n, me, out


def column():
    z, y, item = place()
    n = lax.axis_size("user") // 2
    return n, z, [{"user": 2 * lax.rem(z + o, n) + y, "item": item} for o in range(1, n)]


def facing():
    z, y, item = place()
    return {"user": 2 * z + 1 - y, "item": item}


def meet(devices):
    barrier = pltpu.get_barrier_semaphore()
    for device in devices:
        pl.semaphore_signal(barrier, inc=1, device_id=device, device_id_type=MESH)
    pl.semaphore_wait(barrier, len(devices))


def remote(src, dst, send, recv, device):
    return pltpu.make_async_remote_copy(
        src_ref=src, dst_ref=dst, send_sem=send, recv_sem=recv, device_id=device,
        device_id_type=MESH,
    )


def sum_over(group, value, slots, send, recv, meanwhile=lambda: None):
    n, me, devices = group
    slots[me] = value
    copies = [
        remote(slots.at[me], slots.at[me], send.at[o], recv.at[o], device)
        for o, device in enumerate(devices)
    ]
    for copy in copies:
        copy.start()
    meanwhile()
    for copy in copies:
        copy.wait()
    total = slots[0]
    for i in range(1, n):
        total = total + slots[i]
    return total


def gather_kernel(
    seeds, cat_ref, v_ref, stats_ref, tiles_ref,
    slots_p, slots_c, sp, rp, sc, rc, sz, rz, sy, ry,
):
    groups = tiles_ref.shape[0] // GROUP
    parts = lax.axis_size("user")

    def some(i):
        first, last = (i, i + 1) if i < 2 else (2 * i - 2, 2 * i)
        fill(seeds, tiles_ref, groups * first // parts, groups * last // parts, True)

    nlock = stats_ref.shape[0]
    width = v_ref.shape[1]
    meet(plane()[2] + column()[2])
    lock = cat_ref[:nlock]
    stats = lax.dot_general(lock, cat_ref[...], NT, preferred_element_type=jnp.float32)
    stats = sum_over(plane(), stats, slots_p, sp, rp, lambda: some(0))
    stats = sum_over(column(), stats, slots_c, sc, rc, lambda: some(1))
    stats_ref[...] = stats
    projt = stats.T[nlock : nlock + width]
    own = cat_ref.shape[1] // TILE
    n, z, devices = column()
    y = place()[1]

    def block(o):
        at = (2 * lax.rem(z + n - o, n) + y) * own
        return v_ref.at[pl.ds(at, own)]

    for j in range(own):
        at = slice(j * TILE, (j + 1) * TILE)
        v = cat_ref[nlock : nlock + width, at].astype(jnp.float32)
        part = jnp.dot(projt, cat_ref[:nlock, at].astype(jnp.float32), precision=HIGH)
        v_ref[(2 * z + y) * own + j] = (v - part).astype(v_ref.dtype)
    down = [
        remote(block(0), block(0), sz.at[o], rz.at[o], device)
        for o, device in enumerate(devices)
    ]
    over = [remote(block(o), block(o), sy.at[o], ry.at[o], facing()) for o in range(n)]
    for copy in down:
        copy.start()
    over[0].start()
    for o in range(1, n):
        some(1 + o)
        down[o - 1].wait_recv()
        over[o].start()
    for copy in down:
        copy.wait_send()
    for copy in over:
        copy.wait()


def user_sum_kernel(seeds, part_ref, u_ref, tiles_ref, near, pair, far, sem):
    groups = tiles_ref.shape[0] // GROUP
    early, late = groups // 32, groups * 6 // 32
    me = lax.axis_index("item")
    side = lax.rem(me, 2)
    sibling = {"item": me + 1 - 2 * side}
    across = {"item": lax.rem(me + 2, 4)}
    half = part_ref.shape[0] // 2
    size = half // CHUNKS
    meet([sibling, across])

    def copies(step, src, src_at, dst, dst_at, device):
        return [
            remote(
                src.at[pl.ds(src_at + k * size, size)],
                dst.at[pl.ds(dst_at + k * size, size)],
                sem.at[2 * step, k],
                sem.at[2 * step + 1, k],
                device,
            )
            for k in range(CHUNKS)
        ]

    give = copies(0, part_ref, (1 - side) * half, near, 0, sibling)
    swap = copies(1, pair, 0, far, 0, across)
    back = copies(2, u_ref, side * half, u_ref, side * half, sibling)
    for copy in give:
        copy.start()
    for k in range(CHUNKS):
        give[k].wait_recv()
        at = pl.ds(k * size, size)
        own = part_ref[pl.ds(side * half + k * size, size)].astype(jnp.float32)
        pair[at] = (own + near[at].astype(jnp.float32)).astype(pair.dtype)
        swap[k].start()
        fill(seeds, tiles_ref, k * early, (k + 1) * early, False)
    for k in range(CHUNKS):
        first = CHUNKS * early + k * late
        fill(seeds, tiles_ref, first, first + late, False)
        swap[k].wait_recv()
        at = pl.ds(k * size, size)
        total = pair[at].astype(jnp.float32) + far[at].astype(jnp.float32)
        u_ref[pl.ds(side * half + k * size, size)] = total.astype(u_ref.dtype)
        back[k].start()
    fill(seeds, tiles_ref, CHUNKS * (early + late), groups, False)
    for k in range(CHUNKS):
        give[k].wait_send()
        swap[k].wait_send()
        back[k].wait()


def finish_kernel(
    items, part_ref, lock_ref, stats_ref, v_ref,
    near, pair, land, slots_p, slots_c, sy, ry, sz, rz, sp, rp, sc, rc,
):
    nlock = stats_ref.shape[0]
    own, width, tile = land.shape[1:]
    n, z, devices = column()
    y = place()[1]
    meet(plane()[2] + devices)

    def piece(t, side):
        return pl.ds((2 * lax.rem(z + 1 + t, n) + side) * own, own)

    over = [
        remote(part_ref.at[piece(t, 1 - y)], near.at[t], sy.at[t], ry.at[t], facing())
        for t in range(n)
    ]
    down = [
        remote(pair.at[t], land.at[t], sz.at[t], rz.at[t], device)
        for t, device in enumerate(devices)
    ]
    for copy in over:
        copy.start()
    for t in range(n):
        over[t].wait_recv()
        both = part_ref[piece(t, y)].astype(jnp.float32) + near[t].astype(jnp.float32)
        if t < n - 1:
            pair[t] = both.astype(pair.dtype)
            down[t].start()
    for copy in over:
        copy.wait_send()
    for copy in down:
        copy.wait()
    back, square = [], jnp.zeros((width, tile), jnp.float32)
    rows = nlock + 8
    sums = jnp.zeros((rows, width), jnp.float32)
    for j in range(own):
        b = part_ref[(2 * z + y) * own + j].astype(jnp.float32) + near[n - 1, j].astype(
            jnp.float32
        )
        for t in range(n - 1):
            b = b + land[t, j].astype(jnp.float32)
        back.append(b)
        square = square + b * b
        lock = lock_ref[:rows, j * tile : (j + 1) * tile].astype(jnp.float32)
        sums = sums + lax.dot_general(
            lock, b, NT, precision=HIGH, preferred_element_type=jnp.float32
        )
    squares = lax.dot_general(
        jnp.ones((rows, tile), jnp.float32), square, NT, precision=HIGH,
        preferred_element_type=jnp.float32,
    )
    lane = lax.broadcasted_iota(jnp.int32, (rows, width), 0)
    sums = jnp.where(lane >= nlock, squares, sums)
    sums = jnp.concatenate([sums, jnp.zeros((rows, tile - width), jnp.float32)], axis=1)
    sums = sum_over(plane(), sums, slots_p, sp, rp)
    sums = sum_over(column(), sums, slots_c, sc, rc)
    sums = sums.T[:width]
    proj2, backsq = sums[:, :nlock], sums[:, nlock : nlock + 1]
    gram = stats_ref[:, :nlock]
    crossed = jnp.dot(proj2, gram, precision=HIGH) - 2.0 * proj2
    colsq = backsq + jnp.sum(proj2 * crossed, axis=1, keepdims=True)
    scale = 1.0 / jnp.sqrt(jnp.maximum(colsq, 0.0) / items + 1e-06)
    for j in range(own):
        lock = lock_ref[:nlock, j * tile : (j + 1) * tile].astype(jnp.float32)
        rest = back[j] - jnp.dot(proj2, lock, precision=HIGH)
        v_ref[j * tile : (j + 1) * tile, :] = (rest * scale).T


def comm_call(kernel, name, key, out_shape, scratch, *args):
    vmem = pl.BlockSpec(memory_space=pltpu.VMEM)
    return pl.pallas_call(
        kernel,
        name=name,
        out_shape=out_shape,
        in_specs=[SMEM_SPEC if x.dtype == jnp.int32 else vmem for x in args],
        out_specs=jax.tree.map(lambda _: vmem, out_shape),
        scratch_shapes=scratch,
        compiler_params=pltpu.CompilerParams(
            collective_id=key, has_side_effects=True, vmem_limit_bytes=LIMIT
        ),
    )(*args)


def sems(*shape):
    return pltpu.SemaphoreType.DMA(shape)


def remote_plan(v_start, locked, tile_rows, tile_cols, tile_seeds, tile_count):
    n_user, n_item = lax.axis_size("user"), lax.axis_size("item")
    shard, width = v_start.shape
    nlock = locked.shape[1]
    nblocks = shard * n_user // TILE
    pad = jnp.zeros((shard, TILE - nlock - width), v_start.dtype)
    cat = jnp.concatenate([locked, v_start, pad], axis=1).T
    slab = (nblocks, width, TILE)
    wide, deep = 2 * n_item, n_user // 2
    pair = [sems(wide - 1)] * 2 + [sems(deep - 1)] * 2
    vblocks, stats, tiles = comm_call(
        gather_kernel,
        "gather",
        0,
        (
            jax.ShapeDtypeStruct(slab, jnp.bfloat16),
            jax.ShapeDtypeStruct((nlock, TILE), jnp.float32),
            jax.ShapeDtypeStruct((tile_seeds.shape[1], TILE, TILE), jnp.bfloat16),
        ),
        [
            pltpu.VMEM((wide, nlock, TILE), jnp.float32),
            pltpu.VMEM((deep, nlock, TILE), jnp.float32),
        ]
        + pair
        + [sems(deep - 1)] * 2
        + [sems(deep)] * 2,
        tile_seeds,
        cat,
    )
    places = pack(tile_rows, tile_cols)
    upart = product(True, places, tile_count, vblocks, tiles, RB, jnp.bfloat16)
    half = pltpu.VMEM((RB // 2, width, TILE), jnp.bfloat16)
    ublocks, tiles = comm_call(
        user_sum_kernel,
        "user_sum",
        1,
        (
            jax.ShapeDtypeStruct((RB, width, TILE), jnp.bfloat16),
            jax.ShapeDtypeStruct((tile_seeds.shape[1], TILE, TILE), jnp.bfloat16),
        ),
        [half, half, half, sems(6, CHUNKS)],
        tile_seeds,
        upart,
    )
    wpart = product(False, places, tile_count, ublocks, tiles, nblocks, jnp.bfloat16)
    per = RB // n_item
    u_factor = rows_of(lax.dynamic_slice_in_dim(ublocks, lax.axis_index("item") * per, per, 0))
    only = jnp.concatenate([locked, jnp.zeros((shard, TILE - nlock), locked.dtype)], axis=1).T
    v_next = comm_call(
        functools.partial(finish_kernel, float(shard * n_user * n_item)),
        "finish",
        2,
        jax.ShapeDtypeStruct((shard, width), jnp.float32),
        [
            pltpu.VMEM((deep, nblocks // n_user, width, TILE), jnp.bfloat16),
            pltpu.VMEM((deep - 1, nblocks // n_user, width, TILE), jnp.bfloat16),
            pltpu.VMEM((deep - 1, nblocks // n_user, width, TILE), jnp.bfloat16),
            pltpu.VMEM((wide, nlock + 8, TILE), jnp.float32),
            pltpu.VMEM((deep, nlock + 8, TILE), jnp.float32),
        ]
        + [sems(deep)] * 2
        + [sems(deep - 1)] * 2
        + pair,
        wpart,
        only,
        stats,
    )
    return (u_factor, v_next)


def on_device(v_start, locked, tile_rows, tile_cols, tile_seeds, tile_count):
    if v_start.shape[0] % TILE == 0 and lax.axis_size("item") == 4 and lax.axis_size("user") % 2 == 0:
        return remote_plan(v_start, locked, tile_rows, tile_cols, tile_seeds, tile_count)
    both = ("user", "item")
    lockf = locked.astype(jnp.float32)
    nlock = locked.shape[1]
    n_user, n_item = lax.axis_size("user"), lax.axis_size("item")
    slab = v_start.shape[0] * n_user
    stats = jnp.dot(
        locked.T, jnp.concatenate([v_start, locked], axis=1), preferred_element_type=jnp.float32
    )
    stats = lax.psum(stats, both)
    proj, gram = stats[:, :-nlock], stats[:, -nlock:]
    deflated = (v_start.astype(jnp.float32) - jnp.dot(lockf, proj, precision=HIGH)).astype(
        jnp.bfloat16
    )
    vslab = lax.all_gather(deflated, "user", axis=0, tiled=True)
    places = pack(tile_rows, tile_cols)
    flipped, tiles = [
        pl.pallas_call(
            functools.partial(fill_kernel, flip),
            name="fill",
            out_shape=jax.ShapeDtypeStruct((tile_seeds.shape[1], TILE, TILE), jnp.bfloat16),
            in_specs=[SMEM_SPEC],
            out_specs=VMEM_SPEC,
            compiler_params=pltpu.CompilerParams(vmem_limit_bytes=LIMIT),
        )(tile_seeds)
        for flip in (True, False)
    ]
    upart = product(True, places, tile_count, blocks_of(vslab), flipped, RB, jnp.float32)
    ublocks = lax.psum(upart, "item").astype(jnp.bfloat16)
    per = RB // n_item
    u_factor = rows_of(lax.dynamic_slice_in_dim(ublocks, lax.axis_index("item") * per, per, 0))
    wpart = product(False, places, tile_count, ublocks, tiles, slab // TILE, jnp.float32)
    back = lax.psum_scatter(rows_of(wpart), "user", scatter_dimension=0, tiled=True)
    sums = jnp.concatenate(
        [jnp.dot(lockf.T, back, precision=HIGH), jnp.sum(back * back, axis=0)[None]], axis=0
    )
    sums = lax.psum(sums, both)
    proj2, backsq = sums[:-1], sums[-1]
    rest = back - jnp.dot(lockf, proj2, precision=HIGH)
    crossed = jnp.dot(gram, proj2, precision=HIGH) - 2.0 * proj2
    colsq = jnp.maximum(backsq + jnp.sum(proj2 * crossed, axis=0), 0.0)
    v_next = rest / jnp.sqrt(colsq / (slab * n_item) + 1e-06)
    return (u_factor, v_next)


def solution(mesh):
    spec = P(("user", "item"), None)
    return jax.shard_map(
        on_device, mesh=mesh, in_specs=(spec,) * 6, out_specs=(spec, spec), check_vma=False
    )
```

```python
import functools

import jax
import jax.numpy as jnp
from jax import lax
from jax.experimental import pallas as pl
from jax.experimental.pallas import tpu as pltpu
from jax.sharding import PartitionSpec as P

TILE = 128
RB = 64
LIMIT = 16 << 20
GROUP = 16
SPAN = 64
SCALE = 1.0 / 1024.0
HIGH = lax.Precision.HIGHEST
NT = (((1,), (1,)), ((), ()))
NN = (((1,), (0,)), ((), ()))


def fill(seeds, tiles_ref, first, last, flip):
    a = lax.broadcasted_iota(jnp.int32, (TILE, TILE), 0)
    b = lax.broadcasted_iota(jnp.int32, (TILE, TILE), 1)
    base = (b * TILE + a if flip else a * TILE + b) * 40503

    def step(g, carry):
        for j in range(GROUP):
            s = g * GROUP + j
            h = base + seeds[0, s] * 9973
            h = h ^ (h >> 13)
            h = h * 1597334677
            h = h ^ (h >> 16)
            levels = ((h >> 8) & 255) - 128
            tiles_ref[s] = levels.astype(jnp.float32).astype(jnp.bfloat16)
        return carry

    lax.fori_loop(first, last, step, 0)


def fill_kernel(flip, seeds, tiles_ref):
    fill(seeds, tiles_ref, 0, tiles_ref.shape[0] // GROUP, flip)


def product_kernel(forward, places, count, x_ref, tiles_ref, out_ref, acc):
    blocks = out_ref.shape[0]
    live = count[0, 0]
    acc[...] = jnp.zeros_like(acc)

    def step(g, carry):
        for j in range(SPAN):
            s = g * SPAN + j
            row, col = places[0, s] >> 16, places[0, s] & 65535
            source, target = (col, row) if forward else (row, col)
            target = jnp.where(s < live, target, blocks)
            acc[target] += lax.dot_general(
                x_ref[source], tiles_ref[s], NN, preferred_element_type=jnp.float32
            )
        return carry

    lax.fori_loop(0, lax.div(live + (SPAN - 1), SPAN), step, 0)
    out_ref[...] = (acc[:blocks] * SCALE).astype(out_ref.dtype)


VMEM_SPEC = pl.BlockSpec(memory_space=pltpu.VMEM)
SMEM_SPEC = pl.BlockSpec(memory_space=pltpu.SMEM)


def product(forward, places, count, x, tiles, nblocks, dtype):
    width, tile = x.shape[1:]
    return pl.pallas_call(
        functools.partial(product_kernel, forward),
        name="forward" if forward else "backward",
        out_shape=jax.ShapeDtypeStruct((nblocks, width, tile), dtype),
        in_specs=[SMEM_SPEC, SMEM_SPEC, VMEM_SPEC, VMEM_SPEC],
        out_specs=VMEM_SPEC,
        scratch_shapes=[pltpu.VMEM((nblocks + 1, width, tile), jnp.float32)],
        compiler_params=pltpu.CompilerParams(vmem_limit_bytes=LIMIT),
    )(places, count, x, tiles)


def pack(tile_rows, tile_cols):
    return tile_rows * 65536 + tile_cols


def blocks_of(x):
    return x.reshape(-1, TILE, x.shape[1]).transpose(0, 2, 1)


def rows_of(blocks):
    return blocks.transpose(0, 2, 1).reshape(-1, blocks.shape[1])


MESH = pl.DeviceIdType.MESH
CHUNKS = 8


def place():
    user = lax.axis_index("user")
    return lax.div(user, 2), lax.rem(user, 2), lax.axis_index("item")


def plane():
    z, y, item = place()
    n = 2 * lax.axis_size("item")
    me = y * lax.axis_size("item") + item
    out = []
    for o in range(1, n):
        p = lax.rem(me + o, n)
        out.append({"user": 2 * z + lax.div(p, n // 2), "item": lax.rem(p, n // 2)})
    return n, me, out


def column():
    z, y, item = place()
    n = lax.axis_size("user") // 2
    return n, z, [{"user": 2 * lax.rem(z + o, n) + y, "item": item} for o in range(1, n)]


def facing():
    z, y, item = place()
    return {"user": 2 * z + 1 - y, "item": item}


def meet(devices):
    barrier = pltpu.get_barrier_semaphore()
    for device in devices:
        pl.semaphore_signal(barrier, inc=1, device_id=device, device_id_type=MESH)
    pl.semaphore_wait(barrier, len(devices))


def remote(src, dst, send, recv, device):
    return pltpu.make_async_remote_copy(
        src_ref=src, dst_ref=dst, send_sem=send, recv_sem=recv, device_id=device,
        device_id_type=MESH,
    )


def sum_over(group, value, slots, send, recv, meanwhile=lambda: None):
    n, me, devices = group
    slots[me] = value
    copies = [
        remote(slots.at[me], slots.at[me], send.at[o], recv.at[o], device)
        for o, device in enumerate(devices)
    ]
    for copy in copies:
        copy.start()
    meanwhile()
    for copy in copies:
        copy.wait()
    total = slots[0]
    for i in range(1, n):
        total = total + slots[i]
    return total


def gather_kernel(
    seeds, cat_ref, v_ref, stats_ref, tiles_ref,
    slots_p, slots_c, sp, rp, sc, rc, sz, rz, sy, ry,
):
    groups = tiles_ref.shape[0] // GROUP
    parts = lax.axis_size("user")

    def some(i):
        first, last = (i, i + 1) if i < 2 else (2 * i - 2, 2 * i)
        fill(seeds, tiles_ref, groups * first // parts, groups * last // parts, True)

    nlock = stats_ref.shape[0]
    width = v_ref.shape[1]
    meet(plane()[2] + column()[2])
    lock = cat_ref[:nlock]
    stats = lax.dot_general(lock, cat_ref[...], NT, preferred_element_type=jnp.float32)
    stats = sum_over(plane(), stats, slots_p, sp, rp, lambda: some(0))
    stats = sum_over(column(), stats, slots_c, sc, rc, lambda: some(1))
    stats_ref[...] = stats
    projt = stats.T[nlock : nlock + width]
    own = cat_ref.shape[1] // TILE
    n, z, devices = column()
    y = place()[1]

    def block(o):
        at = (2 * lax.rem(z + n - o, n) + y) * own
        return v_ref.at[pl.ds(at, own)]

    for j in range(own):
        at = slice(j * TILE, (j + 1) * TILE)
        v = cat_ref[nlock : nlock + width, at].astype(jnp.float32)
        part = jnp.dot(projt, cat_ref[:nlock, at].astype(jnp.float32), precision=HIGH)
        v_ref[(2 * z + y) * own + j] = (v - part).astype(v_ref.dtype)
    down = [
        remote(block(0), block(0), sz.at[o], rz.at[o], device)
        for o, device in enumerate(devices)
    ]
    over = [remote(block(o), block(o), sy.at[o], ry.at[o], facing()) for o in range(n)]
    for copy in down:
        copy.start()
    over[0].start()
    for o in range(1, n):
        some(1 + o)
        down[o - 1].wait_recv()
        over[o].start()
    for copy in down:
        copy.wait_send()
    for copy in over:
        copy.wait()


def user_sum_kernel(seeds, part_ref, u_ref, tiles_ref, near, pair, far, sem):
    groups = tiles_ref.shape[0] // GROUP
    early, late = groups // 32, groups * 3 // 32
    me = lax.axis_index("item")
    side = lax.rem(me, 2)
    sibling = {"item": me + 1 - 2 * side}
    across = {"item": lax.rem(me + 2, 4)}
    half = part_ref.shape[0] // 2
    size = half // CHUNKS
    meet([sibling, across])

    def copies(step, src, src_at, dst, dst_at, device):
        return [
            remote(
                src.at[pl.ds(src_at + k * size, size)],
                dst.at[pl.ds(dst_at + k * size, size)],
                sem.at[2 * step, k],
                sem.at[2 * step + 1, k],
                device,
            )
            for k in range(CHUNKS)
        ]

    give = copies(0, part_ref, (1 - side) * half, near, 0, sibling)
    swap = copies(1, pair, 0, far, 0, across)
    back = copies(2, u_ref, side * half, u_ref, side * half, sibling)
    for copy in give:
        copy.start()
    for k in range(CHUNKS):
        give[k].wait_recv()
        at = pl.ds(k * size, size)
        own = part_ref[pl.ds(side * half + k * size, size)].astype(jnp.float32)
        pair[at] = (own + near[at].astype(jnp.float32)).astype(pair.dtype)
        swap[k].start()
        fill(seeds, tiles_ref, k * early, (k + 1) * early, False)
    for k in range(CHUNKS):
        first = CHUNKS * early + k * late
        fill(seeds, tiles_ref, first, first + late, False)
        swap[k].wait_recv()
        at = pl.ds(k * size, size)
        total = pair[at].astype(jnp.float32) + far[at].astype(jnp.float32)
        u_ref[pl.ds(side * half + k * size, size)] = total.astype(u_ref.dtype)
        back[k].start()
    fill(seeds, tiles_ref, CHUNKS * (early + late), groups, False)
    for k in range(CHUNKS):
        give[k].wait_send()
        swap[k].wait_send()
        back[k].wait()


def finish_kernel(
    items, part_ref, lock_ref, stats_ref, v_ref,
    near, pair, land, slots_p, slots_c, sy, ry, sz, rz, sp, rp, sc, rc,
):
    nlock = stats_ref.shape[0]
    own, width, tile = land.shape[1:]
    n, z, devices = column()
    y = place()[1]
    meet(plane()[2] + devices)

    def piece(t, side):
        return pl.ds((2 * lax.rem(z + 1 + t, n) + side) * own, own)

    over = [
        remote(part_ref.at[piece(t, 1 - y)], near.at[t], sy.at[t], ry.at[t], facing())
        for t in range(n)
    ]
    down = [
        remote(pair.at[t], land.at[t], sz.at[t], rz.at[t], device)
        for t, device in enumerate(devices)
    ]
    for copy in over:
        copy.start()
    for t in range(n):
        over[t].wait_recv()
        both = part_ref[piece(t, y)].astype(jnp.float32) + near[t].astype(jnp.float32)
        if t < n - 1:
            pair[t] = both.astype(pair.dtype)
            down[t].start()
    for copy in over:
        copy.wait_send()
    for copy in down:
        copy.wait()
    back, square = [], jnp.zeros((width, tile), jnp.float32)
    rows = nlock + 8
    sums = jnp.zeros((rows, width), jnp.float32)
    for j in range(own):
        b = part_ref[(2 * z + y) * own + j].astype(jnp.float32) + near[n - 1, j].astype(
            jnp.float32
        )
        for t in range(n - 1):
            b = b + land[t, j].astype(jnp.float32)
        back.append(b)
        square = square + b * b
        lock = lock_ref[:rows, j * tile : (j + 1) * tile].astype(jnp.float32)
        sums = sums + lax.dot_general(
            lock, b, NT, precision=HIGH, preferred_element_type=jnp.float32
        )
    squares = lax.dot_general(
        jnp.ones((rows, tile), jnp.float32), square, NT, precision=HIGH,
        preferred_element_type=jnp.float32,
    )
    lane = lax.broadcasted_iota(jnp.int32, (rows, width), 0)
    sums = jnp.where(lane >= nlock, squares, sums)
    sums = jnp.concatenate([sums, jnp.zeros((rows, tile - width), jnp.float32)], axis=1)
    sums = sum_over(plane(), sums, slots_p, sp, rp)
    sums = sum_over(column(), sums, slots_c, sc, rc)
    sums = sums.T[:width]
    proj2, backsq = sums[:, :nlock], sums[:, nlock : nlock + 1]
    gram = stats_ref[:, :nlock]
    crossed = jnp.dot(proj2, gram, precision=HIGH) - 2.0 * proj2
    colsq = backsq + jnp.sum(proj2 * crossed, axis=1, keepdims=True)
    scale = 1.0 / jnp.sqrt(jnp.maximum(colsq, 0.0) / items + 1e-06)
    for j in range(own):
        lock = lock_ref[:nlock, j * tile : (j + 1) * tile].astype(jnp.float32)
        rest = back[j] - jnp.dot(proj2, lock, precision=HIGH)
        v_ref[j * tile : (j + 1) * tile, :] = (rest * scale).T


def comm_call(kernel, name, key, out_shape, scratch, *args):
    vmem = pl.BlockSpec(memory_space=pltpu.VMEM)
    return pl.pallas_call(
        kernel,
        name=name,
        out_shape=out_shape,
        in_specs=[SMEM_SPEC if x.dtype == jnp.int32 else vmem for x in args],
        out_specs=jax.tree.map(lambda _: vmem, out_shape),
        scratch_shapes=scratch,
        compiler_params=pltpu.CompilerParams(
            collective_id=key, has_side_effects=True, vmem_limit_bytes=LIMIT
        ),
    )(*args)


def sems(*shape):
    return pltpu.SemaphoreType.DMA(shape)


def remote_plan(v_start, locked, tile_rows, tile_cols, tile_seeds, tile_count):
    n_user, n_item = lax.axis_size("user"), lax.axis_size("item")
    shard, width = v_start.shape
    nlock = locked.shape[1]
    nblocks = shard * n_user // TILE
    pad = jnp.zeros((shard, TILE - nlock - width), v_start.dtype)
    cat = jnp.concatenate([locked, v_start, pad], axis=1).T
    slab = (nblocks, width, TILE)
    wide, deep = 2 * n_item, n_user // 2
    pair = [sems(wide - 1)] * 2 + [sems(deep - 1)] * 2
    vblocks, stats, tiles = comm_call(
        gather_kernel,
        "gather",
        0,
        (
            jax.ShapeDtypeStruct(slab, jnp.bfloat16),
            jax.ShapeDtypeStruct((nlock, TILE), jnp.float32),
            jax.ShapeDtypeStruct((tile_seeds.shape[1], TILE, TILE), jnp.bfloat16),
        ),
        [
            pltpu.VMEM((wide, nlock, TILE), jnp.float32),
            pltpu.VMEM((deep, nlock, TILE), jnp.float32),
        ]
        + pair
        + [sems(deep - 1)] * 2
        + [sems(deep)] * 2,
        tile_seeds,
        cat,
    )
    places = pack(tile_rows, tile_cols)
    upart = product(True, places, tile_count, vblocks, tiles, RB, jnp.bfloat16)
    half = pltpu.VMEM((RB // 2, width, TILE), jnp.bfloat16)
    ublocks, tiles = comm_call(
        user_sum_kernel,
        "user_sum",
        1,
        (
            jax.ShapeDtypeStruct((RB, width, TILE), jnp.bfloat16),
            jax.ShapeDtypeStruct((tile_seeds.shape[1], TILE, TILE), jnp.bfloat16),
        ),
        [half, half, half, sems(6, CHUNKS)],
        tile_seeds,
        upart,
    )
    wpart = product(False, places, tile_count, ublocks, tiles, nblocks, jnp.bfloat16)
    per = RB // n_item
    u_factor = rows_of(lax.dynamic_slice_in_dim(ublocks, lax.axis_index("item") * per, per, 0))
    only = jnp.concatenate([locked, jnp.zeros((shard, TILE - nlock), locked.dtype)], axis=1).T
    v_next = comm_call(
        functools.partial(finish_kernel, float(shard * n_user * n_item)),
        "finish",
        2,
        jax.ShapeDtypeStruct((shard, width), jnp.float32),
        [
            pltpu.VMEM((deep, nblocks // n_user, width, TILE), jnp.bfloat16),
            pltpu.VMEM((deep - 1, nblocks // n_user, width, TILE), jnp.bfloat16),
            pltpu.VMEM((deep - 1, nblocks // n_user, width, TILE), jnp.bfloat16),
            pltpu.VMEM((wide, nlock + 8, TILE), jnp.float32),
            pltpu.VMEM((deep, nlock + 8, TILE), jnp.float32),
        ]
        + [sems(deep)] * 2
        + [sems(deep - 1)] * 2
        + pair,
        wpart,
        only,
        stats,
    )
    return (u_factor, v_next)


def on_device(v_start, locked, tile_rows, tile_cols, tile_seeds, tile_count):
    if v_start.shape[0] % TILE == 0 and lax.axis_size("item") == 4 and lax.axis_size("user") % 2 == 0:
        return remote_plan(v_start, locked, tile_rows, tile_cols, tile_seeds, tile_count)
    both = ("user", "item")
    lockf = locked.astype(jnp.float32)
    nlock = locked.shape[1]
    n_user, n_item = lax.axis_size("user"), lax.axis_size("item")
    slab = v_start.shape[0] * n_user
    stats = jnp.dot(
        locked.T, jnp.concatenate([v_start, locked], axis=1), preferred_element_type=jnp.float32
    )
    stats = lax.psum(stats, both)
    proj, gram = stats[:, :-nlock], stats[:, -nlock:]
    deflated = (v_start.astype(jnp.float32) - jnp.dot(lockf, proj, precision=HIGH)).astype(
        jnp.bfloat16
    )
    vslab = lax.all_gather(deflated, "user", axis=0, tiled=True)
    places = pack(tile_rows, tile_cols)
    flipped, tiles = [
        pl.pallas_call(
            functools.partial(fill_kernel, flip),
            name="fill",
            out_shape=jax.ShapeDtypeStruct((tile_seeds.shape[1], TILE, TILE), jnp.bfloat16),
            in_specs=[SMEM_SPEC],
            out_specs=VMEM_SPEC,
            compiler_params=pltpu.CompilerParams(vmem_limit_bytes=LIMIT),
        )(tile_seeds)
        for flip in (True, False)
    ]
    upart = product(True, places, tile_count, blocks_of(vslab), flipped, RB, jnp.float32)
    ublocks = lax.psum(upart, "item").astype(jnp.bfloat16)
    per = RB // n_item
    u_factor = rows_of(lax.dynamic_slice_in_dim(ublocks, lax.axis_index("item") * per, per, 0))
    wpart = product(False, places, tile_count, ublocks, tiles, slab // TILE, jnp.float32)
    back = lax.psum_scatter(rows_of(wpart), "user", scatter_dimension=0, tiled=True)
    sums = jnp.concatenate(
        [jnp.dot(lockf.T, back, precision=HIGH), jnp.sum(back * back, axis=0)[None]], axis=0
    )
    sums = lax.psum(sums, both)
    proj2, backsq = sums[:-1], sums[-1]
    rest = back - jnp.dot(lockf, proj2, precision=HIGH)
    crossed = jnp.dot(gram, proj2, precision=HIGH) - 2.0 * proj2
    colsq = jnp.maximum(backsq + jnp.sum(proj2 * crossed, axis=0), 0.0)
    v_next = rest / jnp.sqrt(colsq / (slab * n_item) + 1e-06)
    return (u_factor, v_next)


def solution(mesh):
    spec = P(("user", "item"), None)
    return jax.shard_map(
        on_device, mesh=mesh, in_specs=(spec,) * 6, out_specs=(spec, spec), check_vma=False
    )
```

```python
import functools

import jax
import jax.numpy as jnp
from jax import lax
from jax.experimental import pallas as pl
from jax.experimental.pallas import tpu as pltpu
from jax.sharding import PartitionSpec as P

TILE = 128
RB = 64
LIMIT = 16 << 20
GROUP = 16
SPAN = 128
SCALE = 1.0 / 1024.0
HIGH = lax.Precision.HIGHEST
NT = (((1,), (1,)), ((), ()))
NN = (((1,), (0,)), ((), ()))


def fill(seeds, tiles_ref, first, last, flip):
    a = lax.broadcasted_iota(jnp.int32, (TILE, TILE), 0)
    b = lax.broadcasted_iota(jnp.int32, (TILE, TILE), 1)
    base = (b * TILE + a if flip else a * TILE + b) * 40503

    def step(g, carry):
        for j in range(GROUP):
            s = g * GROUP + j
            h = base + seeds[0, s] * 9973
            h = h ^ (h >> 13)
            h = h * 1597334677
            h = h ^ (h >> 16)
            levels = ((h >> 8) & 255) - 128
            tiles_ref[s] = levels.astype(jnp.float32).astype(jnp.bfloat16)
        return carry

    lax.fori_loop(first, last, step, 0)


def fill_kernel(flip, seeds, tiles_ref):
    fill(seeds, tiles_ref, 0, tiles_ref.shape[0] // GROUP, flip)


def product_kernel(forward, places, count, x_ref, tiles_ref, out_ref, acc):
    blocks = out_ref.shape[0]
    live = count[0, 0]
    acc[...] = jnp.zeros_like(acc)

    def step(g, carry):
        for j in range(SPAN):
            s = g * SPAN + j
            row, col = places[0, s] >> 16, places[0, s] & 65535
            source, target = (col, row) if forward else (row, col)
            target = jnp.where(s < live, target, blocks)
            acc[target] += lax.dot_general(
                x_ref[source], tiles_ref[s], NN, preferred_element_type=jnp.float32
            )
        return carry

    lax.fori_loop(0, lax.div(live + (SPAN - 1), SPAN), step, 0)
    out_ref[...] = (acc[:blocks] * SCALE).astype(out_ref.dtype)


VMEM_SPEC = pl.BlockSpec(memory_space=pltpu.VMEM)
SMEM_SPEC = pl.BlockSpec(memory_space=pltpu.SMEM)


def product(forward, places, count, x, tiles, nblocks, dtype):
    width, tile = x.shape[1:]
    return pl.pallas_call(
        functools.partial(product_kernel, forward),
        name="forward" if forward else "backward",
        out_shape=jax.ShapeDtypeStruct((nblocks, width, tile), dtype),
        in_specs=[SMEM_SPEC, SMEM_SPEC, VMEM_SPEC, VMEM_SPEC],
        out_specs=VMEM_SPEC,
        scratch_shapes=[pltpu.VMEM((nblocks + 1, width, tile), jnp.float32)],
        compiler_params=pltpu.CompilerParams(vmem_limit_bytes=LIMIT),
    )(places, count, x, tiles)


def pack(tile_rows, tile_cols):
    return tile_rows * 65536 + tile_cols


def blocks_of(x):
    return x.reshape(-1, TILE, x.shape[1]).transpose(0, 2, 1)


def rows_of(blocks):
    return blocks.transpose(0, 2, 1).reshape(-1, blocks.shape[1])


MESH = pl.DeviceIdType.MESH
CHUNKS = 4


def place():
    user = lax.axis_index("user")
    return lax.div(user, 2), lax.rem(user, 2), lax.axis_index("item")


def plane():
    z, y, item = place()
    n = 2 * lax.axis_size("item")
    me = y * lax.axis_size("item") + item
    out = []
    for o in range(1, n):
        p = lax.rem(me + o, n)
        out.append({"user": 2 * z + lax.div(p, n // 2), "item": lax.rem(p, n // 2)})
    return n, me, out


def column():
    z, y, item = place()
    n = lax.axis_size("user") // 2
    return n, z, [{"user": 2 * lax.rem(z + o, n) + y, "item": item} for o in range(1, n)]


def facing():
    z, y, item = place()
    return {"user": 2 * z + 1 - y, "item": item}


def meet(devices):
    barrier = pltpu.get_barrier_semaphore()
    for device in devices:
        pl.semaphore_signal(barrier, inc=1, device_id=device, device_id_type=MESH)
    pl.semaphore_wait(barrier, len(devices))


def remote(src, dst, send, recv, device):
    return pltpu.make_async_remote_copy(
        src_ref=src, dst_ref=dst, send_sem=send, recv_sem=recv, device_id=device,
        device_id_type=MESH,
    )


def sum_over(group, value, slots, send, recv, meanwhile=lambda: None):
    n, me, devices = group
    slots[me] = value
    copies = [
        remote(slots.at[me], slots.at[me], send.at[o], recv.at[o], device)
        for o, device in enumerate(devices)
    ]
    for copy in copies:
        copy.start()
    meanwhile()
    for copy in copies:
        copy.wait()
    total = slots[0]
    for i in range(1, n):
        total = total + slots[i]
    return total


def gather_kernel(
    seeds, cat_ref, v_ref, stats_ref, tiles_ref,
    slots_p, slots_c, sp, rp, sc, rc, sz, rz, sy, ry,
):
    groups = tiles_ref.shape[0] // GROUP
    parts = lax.axis_size("user")

    def some(i):
        first, last = (i, i + 1) if i < 2 else (2 * i - 2, 2 * i)
        fill(seeds, tiles_ref, groups * first // parts, groups * last // parts, True)

    nlock = stats_ref.shape[0]
    width = v_ref.shape[1]
    meet(plane()[2] + column()[2])
    lock = cat_ref[:nlock]
    stats = lax.dot_general(lock, cat_ref[...], NT, preferred_element_type=jnp.float32)
    stats = sum_over(plane(), stats, slots_p, sp, rp, lambda: some(0))
    stats = sum_over(column(), stats, slots_c, sc, rc, lambda: some(1))
    stats_ref[...] = stats
    projt = stats.T[nlock : nlock + width]
    own = cat_ref.shape[1] // TILE
    n, z, devices = column()
    y = place()[1]

    def block(o):
        at = (2 * lax.rem(z + n - o, n) + y) * own
        return v_ref.at[pl.ds(at, own)]

    for j in range(own):
        at = slice(j * TILE, (j + 1) * TILE)
        v = cat_ref[nlock : nlock + width, at].astype(jnp.float32)
        part = jnp.dot(projt, cat_ref[:nlock, at].astype(jnp.float32), precision=HIGH)
        v_ref[(2 * z + y) * own + j] = (v - part).astype(v_ref.dtype)
    down = [
        remote(block(0), block(0), sz.at[o], rz.at[o], device)
        for o, device in enumerate(devices)
    ]
    over = [remote(block(o), block(o), sy.at[o], ry.at[o], facing()) for o in range(n)]
    for copy in down:
        copy.start()
    over[0].start()
    for o in range(1, n):
        some(1 + o)
        down[o - 1].wait_recv()
        over[o].start()
    for copy in down:
        copy.wait_send()
    for copy in over:
        copy.wait()


def user_sum_kernel(seeds, part_ref, u_ref, tiles_ref, near, pair, far, sem):
    groups = tiles_ref.shape[0] // GROUP
    early, late = groups // 32, groups * 6 // 32
    me = lax.axis_index("item")
    side = lax.rem(me, 2)
    sibling = {"item": me + 1 - 2 * side}
    across = {"item": lax.rem(me + 2, 4)}
    half = part_ref.shape[0] // 2
    size = half // CHUNKS
    meet([sibling, across])

    def copies(step, src, src_at, dst, dst_at, device):
        return [
            remote(
                src.at[pl.ds(src_at + k * size, size)],
                dst.at[pl.ds(dst_at + k * size, size)],
                sem.at[2 * step, k],
                sem.at[2 * step + 1, k],
                device,
            )
            for k in range(CHUNKS)
        ]

    give = copies(0, part_ref, (1 - side) * half, near, 0, sibling)
    swap = copies(1, pair, 0, far, 0, across)
    back = copies(2, u_ref, side * half, u_ref, side * half, sibling)
    for copy in give:
        copy.start()
    for k in range(CHUNKS):
        give[k].wait_recv()
        at = pl.ds(k * size, size)
        own = part_ref[pl.ds(side * half + k * size, size)].astype(jnp.float32)
        pair[at] = (own + near[at].astype(jnp.float32)).astype(pair.dtype)
        swap[k].start()
        fill(seeds, tiles_ref, k * early, (k + 1) * early, False)
    for k in range(CHUNKS):
        first = CHUNKS * early + k * late
        fill(seeds, tiles_ref, first, first + late, False)
        swap[k].wait_recv()
        at = pl.ds(k * size, size)
        total = pair[at].astype(jnp.float32) + far[at].astype(jnp.float32)
        u_ref[pl.ds(side * half + k * size, size)] = total.astype(u_ref.dtype)
        back[k].start()
    fill(seeds, tiles_ref, CHUNKS * (early + late), groups, False)
    for k in range(CHUNKS):
        give[k].wait_send()
        swap[k].wait_send()
        back[k].wait()


def finish_kernel(
    items, part_ref, lock_ref, stats_ref, v_ref,
    near, pair, land, slots_p, slots_c, sy, ry, sz, rz, sp, rp, sc, rc,
):
    nlock = stats_ref.shape[0]
    own, width, tile = land.shape[1:]
    n, z, devices = column()
    y = place()[1]
    meet(plane()[2] + devices)

    def piece(t, side):
        return pl.ds((2 * lax.rem(z + 1 + t, n) + side) * own, own)

    over = [
        remote(part_ref.at[piece(t, 1 - y)], near.at[t], sy.at[t], ry.at[t], facing())
        for t in range(n)
    ]
    down = [
        remote(pair.at[t], land.at[t], sz.at[t], rz.at[t], device)
        for t, device in enumerate(devices)
    ]
    for copy in over:
        copy.start()
    for t in range(n):
        over[t].wait_recv()
        both = part_ref[piece(t, y)].astype(jnp.float32) + near[t].astype(jnp.float32)
        if t < n - 1:
            pair[t] = both.astype(pair.dtype)
            down[t].start()
    for copy in over:
        copy.wait_send()
    for copy in down:
        copy.wait()
    back, square = [], jnp.zeros((width, tile), jnp.float32)
    rows = nlock + 8
    sums = jnp.zeros((rows, width), jnp.float32)
    for j in range(own):
        b = part_ref[(2 * z + y) * own + j].astype(jnp.float32) + near[n - 1, j].astype(
            jnp.float32
        )
        for t in range(n - 1):
            b = b + land[t, j].astype(jnp.float32)
        back.append(b)
        square = square + b * b
        lock = lock_ref[:rows, j * tile : (j + 1) * tile].astype(jnp.float32)
        sums = sums + lax.dot_general(
            lock, b, NT, precision=HIGH, preferred_element_type=jnp.float32
        )
    squares = lax.dot_general(
        jnp.ones((rows, tile), jnp.float32), square, NT, precision=HIGH,
        preferred_element_type=jnp.float32,
    )
    lane = lax.broadcasted_iota(jnp.int32, (rows, width), 0)
    sums = jnp.where(lane >= nlock, squares, sums)
    sums = jnp.concatenate([sums, jnp.zeros((rows, tile - width), jnp.float32)], axis=1)
    sums = sum_over(plane(), sums, slots_p, sp, rp)
    sums = sum_over(column(), sums, slots_c, sc, rc)
    sums = sums.T[:width]
    proj2, backsq = sums[:, :nlock], sums[:, nlock : nlock + 1]
    gram = stats_ref[:, :nlock]
    crossed = jnp.dot(proj2, gram, precision=HIGH) - 2.0 * proj2
    colsq = backsq + jnp.sum(proj2 * crossed, axis=1, keepdims=True)
    scale = 1.0 / jnp.sqrt(jnp.maximum(colsq, 0.0) / items + 1e-06)
    for j in range(own):
        lock = lock_ref[:nlock, j * tile : (j + 1) * tile].astype(jnp.float32)
        rest = back[j] - jnp.dot(proj2, lock, precision=HIGH)
        v_ref[j * tile : (j + 1) * tile, :] = (rest * scale).T


def comm_call(kernel, name, key, out_shape, scratch, *args):
    vmem = pl.BlockSpec(memory_space=pltpu.VMEM)
    return pl.pallas_call(
        kernel,
        name=name,
        out_shape=out_shape,
        in_specs=[SMEM_SPEC if x.dtype == jnp.int32 else vmem for x in args],
        out_specs=jax.tree.map(lambda _: vmem, out_shape),
        scratch_shapes=scratch,
        compiler_params=pltpu.CompilerParams(
            collective_id=key, has_side_effects=True, vmem_limit_bytes=LIMIT
        ),
    )(*args)


def sems(*shape):
    return pltpu.SemaphoreType.DMA(shape)


def remote_plan(v_start, locked, tile_rows, tile_cols, tile_seeds, tile_count):
    n_user, n_item = lax.axis_size("user"), lax.axis_size("item")
    shard, width = v_start.shape
    nlock = locked.shape[1]
    nblocks = shard * n_user // TILE
    pad = jnp.zeros((shard, TILE - nlock - width), v_start.dtype)
    cat = jnp.concatenate([locked, v_start, pad], axis=1).T
    slab = (nblocks, width, TILE)
    wide, deep = 2 * n_item, n_user // 2
    pair = [sems(wide - 1)] * 2 + [sems(deep - 1)] * 2
    vblocks, stats, tiles = comm_call(
        gather_kernel,
        "gather",
        0,
        (
            jax.ShapeDtypeStruct(slab, jnp.bfloat16),
            jax.ShapeDtypeStruct((nlock, TILE), jnp.float32),
            jax.ShapeDtypeStruct((tile_seeds.shape[1], TILE, TILE), jnp.bfloat16),
        ),
        [
            pltpu.VMEM((wide, nlock, TILE), jnp.float32),
            pltpu.VMEM((deep, nlock, TILE), jnp.float32),
        ]
        + pair
        + [sems(deep - 1)] * 2
        + [sems(deep)] * 2,
        tile_seeds,
        cat,
    )
    places = pack(tile_rows, tile_cols)
    upart = product(True, places, tile_count, vblocks, tiles, RB, jnp.bfloat16)
    half = pltpu.VMEM((RB // 2, width, TILE), jnp.bfloat16)
    ublocks, tiles = comm_call(
        user_sum_kernel,
        "user_sum",
        1,
        (
            jax.ShapeDtypeStruct((RB, width, TILE), jnp.bfloat16),
            jax.ShapeDtypeStruct((tile_seeds.shape[1], TILE, TILE), jnp.bfloat16),
        ),
        [half, half, half, sems(6, CHUNKS)],
        tile_seeds,
        upart,
    )
    wpart = product(False, places, tile_count, ublocks, tiles, nblocks, jnp.bfloat16)
    per = RB // n_item
    u_factor = rows_of(lax.dynamic_slice_in_dim(ublocks, lax.axis_index("item") * per, per, 0))
    only = jnp.concatenate([locked, jnp.zeros((shard, TILE - nlock), locked.dtype)], axis=1).T
    v_next = comm_call(
        functools.partial(finish_kernel, float(shard * n_user * n_item)),
        "finish",
        2,
        jax.ShapeDtypeStruct((shard, width), jnp.float32),
        [
            pltpu.VMEM((deep, nblocks // n_user, width, TILE), jnp.bfloat16),
            pltpu.VMEM((deep - 1, nblocks // n_user, width, TILE), jnp.bfloat16),
            pltpu.VMEM((deep - 1, nblocks // n_user, width, TILE), jnp.bfloat16),
            pltpu.VMEM((wide, nlock + 8, TILE), jnp.float32),
            pltpu.VMEM((deep, nlock + 8, TILE), jnp.float32),
        ]
        + [sems(deep)] * 2
        + [sems(deep - 1)] * 2
        + pair,
        wpart,
        only,
        stats,
    )
    return (u_factor, v_next)


def on_device(v_start, locked, tile_rows, tile_cols, tile_seeds, tile_count):
    if v_start.shape[0] % TILE == 0 and lax.axis_size("item") == 4 and lax.axis_size("user") % 2 == 0:
        return remote_plan(v_start, locked, tile_rows, tile_cols, tile_seeds, tile_count)
    both = ("user", "item")
    lockf = locked.astype(jnp.float32)
    nlock = locked.shape[1]
    n_user, n_item = lax.axis_size("user"), lax.axis_size("item")
    slab = v_start.shape[0] * n_user
    stats = jnp.dot(
        locked.T, jnp.concatenate([v_start, locked], axis=1), preferred_element_type=jnp.float32
    )
    stats = lax.psum(stats, both)
    proj, gram = stats[:, :-nlock], stats[:, -nlock:]
    deflated = (v_start.astype(jnp.float32) - jnp.dot(lockf, proj, precision=HIGH)).astype(
        jnp.bfloat16
    )
    vslab = lax.all_gather(deflated, "user", axis=0, tiled=True)
    places = pack(tile_rows, tile_cols)
    flipped, tiles = [
        pl.pallas_call(
            functools.partial(fill_kernel, flip),
            name="fill",
            out_shape=jax.ShapeDtypeStruct((tile_seeds.shape[1], TILE, TILE), jnp.bfloat16),
            in_specs=[SMEM_SPEC],
            out_specs=VMEM_SPEC,
            compiler_params=pltpu.CompilerParams(vmem_limit_bytes=LIMIT),
        )(tile_seeds)
        for flip in (True, False)
    ]
    upart = product(True, places, tile_count, blocks_of(vslab), flipped, RB, jnp.float32)
    ublocks = lax.psum(upart, "item").astype(jnp.bfloat16)
    per = RB // n_item
    u_factor = rows_of(lax.dynamic_slice_in_dim(ublocks, lax.axis_index("item") * per, per, 0))
    wpart = product(False, places, tile_count, ublocks, tiles, slab // TILE, jnp.float32)
    back = lax.psum_scatter(rows_of(wpart), "user", scatter_dimension=0, tiled=True)
    sums = jnp.concatenate(
        [jnp.dot(lockf.T, back, precision=HIGH), jnp.sum(back * back, axis=0)[None]], axis=0
    )
    sums = lax.psum(sums, both)
    proj2, backsq = sums[:-1], sums[-1]
    rest = back - jnp.dot(lockf, proj2, precision=HIGH)
    crossed = jnp.dot(gram, proj2, precision=HIGH) - 2.0 * proj2
    colsq = jnp.maximum(backsq + jnp.sum(proj2 * crossed, axis=0), 0.0)
    v_next = rest / jnp.sqrt(colsq / (slab * n_item) + 1e-06)
    return (u_factor, v_next)


def solution(mesh):
    spec = P(("user", "item"), None)
    return jax.shard_map(
        on_device, mesh=mesh, in_specs=(spec,) * 6, out_specs=(spec, spec), check_vma=False
    )
```
